32 devices in a mesh: dp: 8 (over z, y), mp: 4 (over x, core).
Axes of the slice: x: 2, y: 2, z: 4, core: 2. Of those that a mesh axis runs over, the one named last changes fastest.
Arguments:
- hidden: bfloat16 [16384, 768], P(('dp', 'mp')), may hold values from -6 to 6
- segment_ids: int32 [32, 512], P('dp'), may hold values from 0 to 15, never falling along the last dimension, each value on 1 to 64 neighbouring positions
- pad_mask: int32 [32, 512], P('dp'), may hold values 0 or 1
- query_weight: bfloat16 [768, 768], P(None, 'mp'), may hold values from -0.21875 to 0.21875
- query_bias: bfloat16 [768], P('mp'), may hold values from -3 to 3
- key_weight: bfloat16 [768, 768], P(None, 'mp'), may hold values from -0.21875 to 0.21875
- value_weight: bfloat16 [768, 768], P(None, 'mp'), may hold values from -0.21875 to 0.21875
- value_bias: bfloat16 [768], P('mp'), may hold values from -3 to 3
- proj_weight: bfloat16 [768, 768], P('mp'), may hold values from -1.25 to 1.25
- proj_bias: bfloat16 [768], replicated, may hold values from -3 to 3
- norm1_gain: bfloat16 [768], replicated, may hold values from 0.25 to 1.75
- norm1_bias: bfloat16 [768], replicated, may hold values from -3 to 3
- inner_weight: bfloat16 [768, 3072], P(None, 'mp'), may hold values from -0.21875 to 0.21875
- inner_bias: bfloat16 [3072], P('mp'), may hold values from -3 to 3
- outer_weight: bfloat16 [3072, 768], P('mp'), may hold values from -0.15625 to 0.15625
- outer_bias: bfloat16 [768], replicated, may hold values from -3 to 3
- norm2_gain: bfloat16 [768], replicated, may hold values from 0.25 to 1.75
- norm2_bias: bfloat16 [768], replicated, may hold values from -3 to 3
- output_grad: bfloat16 [16384, 768], P(('dp', 'mp')), may hold values from -6 to 6
Outputs:
- output: bfloat16 [16384, 768], P(('dp', 'mp'))
- input_grad: float32 [16384, 768], P(('dp', 'mp'))
- query_weight_grad: float32 [768, 768], P(None, 'mp')
- query_bias_grad: float32 [768], P('mp')
- key_weight_grad: float32 [768, 768], P(None, 'mp')
- value_weight_grad: float32 [768, 768], P(None, 'mp')
- value_bias_grad: float32 [768], P('mp')
- proj_weight_grad: float32 [768, 768], P('mp')
- proj_bias_grad: float32 [768], replicated
- norm1_gain_grad: float32 [768], replicated
- norm1_bias_grad: float32 [768], replicated
- inner_weight_grad: float32 [768, 3072], P(None, 'mp')
- inner_bias_grad: float32 [3072], P('mp')
- outer_weight_grad: float32 [3072, 768], P('mp')
- outer_bias_grad: float32 [768], replicated
- norm2_gain_grad: float32 [768], replicated
- norm2_bias_grad: float32 [768], replicated
The draws below stay inside these ranges and needn't reach their ends.
Inputs may be any that keep to these rules, and one draw needn't show every extreme that they name: `segment_ids`: within a row the ids never fall; a text has 1 to 64 tokens.
All inputs are finite; a program needn't handle non-finite values. No bound on the sum of `pad_mask` on one device may be relied on, other than what follows from the above.
Results may differ from the reference program's by a relative error of at most 0.015.
Values may be sent and summed in bfloat16 or wider, within the bound.
No kernel may reach another device: no remote copies, remote signals or barrier semaphores. Data moves between devices by JAX's collectives and lax.ppermute only.
A program may use at most 128 MiB of HBM per device.

```python
import math
import jax
import jax.numpy as jnp
import numpy as np
from jax import lax

D = 768
HEADS = 12
HD = 64
FF = 3072
SEQ = 512
ROWS = 32
TOKENS = 16384
NSEG = 16
MOST = 64


def place_ends(entries, stream_key, low, largest):
    longest = entries.shape.index(max(entries.shape))
    spots = []
    for shift in (0, 1):
        where = [jax.random.randint(jax.random.fold_in(stream_key, axis), (), 0, length) for axis, length in enumerate(entries.shape)]
        where[longest] = (where[longest] + shift) % entries.shape[longest]
        spots.append(tuple(where))
    return entries.at[spots[0]].set(low).at[spots[1]].set(largest)


def levels(key, dims, cuts, least, top_value):
    level = 1.0
    for dim, blocks in cuts:
        draws = jax.random.uniform(jax.random.fold_in(jax.random.fold_in(key, 6), dim), (blocks,), jnp.float32, least / len(cuts), top_value / len(cuts))
        level = level * jnp.repeat(jnp.exp(draws), dims[dim] // blocks).reshape((-1,) + (1,) * (len(dims) - 1 - dim))
    return level


def split_up(amount, total, bound, slope):
    weights = [(1 << 20) // math.isqrt(rank ** slope) + 1 for rank in range(2, amount + 1)]
    spare, holding = total - bound - (amount - 1), [1] * (amount - 1)
    while spare > 0:
        movable = [i for i in range(amount - 1) if holding[i] < bound]
        mass, budget = sum([weights[i] for i in movable]), spare
        for i in movable:
            more = min(bound - holding[i], max(1, budget * weights[i] // mass), spare)
            holding[i] = holding[i] + more
            spare = spare - more
    return np.array([bound] + holding)


def ragged(key, count, total, most, lean):
    if count == 2:
        one = jax.random.randint(key, (), max(1, total - most), min(most, total - 1) + 1)
        return jnp.stack([one, total - one])
    lengths = jnp.asarray(split_up(count, total, most, lean), jnp.int32)
    twos = (count - 1) // 2
    donor, receiver = lengths[1:1 + 2 * twos:2], lengths[2:2 + 2 * twos:2]
    slack = jnp.minimum(donor - 1, most - receiver)
    passed = jax.random.randint(jax.random.fold_in(key, 1), (twos,), 0, 1 << 20) % (slack + 1)
    lengths = lengths.at[1:1 + 2 * twos:2].set(donor - passed).at[2:2 + 2 * twos:2].set(receiver + passed)
    return lengths[jax.random.permutation(jax.random.fold_in(key, 2), count)]


def centred(own_key, shape, scale, reach, shards=(), kind=jnp.bfloat16):
    entries = jax.random.normal(own_key, shape, jnp.float32) * scale
    if len(shards) > 0:
        entries = levels(own_key, shape, shards, -0.22, 0.18) * entries
    return jnp.clip(entries, min=-reach, max=reach).astype(kind)


def setup_inputs(seed: int = 0) -> dict:
    seeds = jax.random.split(jax.random.key(seed), 20)
    hidden = centred(seeds[0], (TOKENS, D), 1.0, 6.0, ((0, 32),))
    segment_ids = jax.vmap(lambda own: jnp.searchsorted(jnp.cumsum(ragged(own, NSEG, SEQ, MOST, 1)), jnp.arange(SEQ), side="right"))(jax.random.split(seeds[1], ROWS)).reshape((ROWS, SEQ)).astype(jnp.int32)
    pad_mask = place_ends((jax.random.randint(seeds[2], (ROWS, SEQ), 0, 16) < 15).astype(jnp.int32), jax.random.fold_in(seeds[2], 1), 0, 1)
    query_weight = centred(seeds[3], (D, D), D ** -0.5, 0.21875, ((1, 4),))
    query_bias = centred(seeds[4], (D,), 0.5, 3.0, ((0, 4),))
    key_weight = centred(seeds[5], (D, D), D ** -0.5, 0.21875, ((1, 4),))
    value_weight = centred(seeds[6], (D, D), D ** -0.5, 0.21875, ((1, 4),))
    value_bias = centred(seeds[7], (D,), 0.5, 3.0, ((0, 4),))
    proj_weight = centred(seeds[8], (D, D), (D // 32) ** -0.5, 1.25, ((0, 4),))
    proj_bias = centred(seeds[9], (D,), 0.5, 3.0)
    norm1_gain = jnp.clip(1.0 + 0.15 * jax.random.normal(seeds[10], (D,), jnp.float32), 0.25, 1.75).astype(jnp.bfloat16)
    norm1_bias = centred(seeds[11], (D,), 0.5, 3.0)
    inner_weight = centred(seeds[12], (D, FF), D ** -0.5, 0.21875, ((1, 4),))
    inner_bias = centred(seeds[13], (FF,), 0.5, 3.0, ((0, 4),))
    outer_weight = centred(seeds[14], (FF, D), (FF // 2) ** -0.5, 0.15625, ((0, 4),))
    outer_bias = centred(seeds[15], (D,), 0.5, 3.0)
    norm2_gain = jnp.clip(1.0 + 0.15 * jax.random.normal(seeds[16], (D,), jnp.float32), 0.25, 1.75).astype(jnp.bfloat16)
    norm2_bias = centred(seeds[17], (D,), 0.5, 3.0)
    output_grad = centred(seeds[18], (TOKENS, D), 1.0, 6.0, ((0, 32),))
    return {"hidden": hidden, "segment_ids": segment_ids, "pad_mask": pad_mask, "query_weight": query_weight, "query_bias": query_bias, "key_weight": key_weight, "value_weight": value_weight, "value_bias": value_bias, "proj_weight": proj_weight, "proj_bias": proj_bias, "norm1_gain": norm1_gain, "norm1_bias": norm1_bias, "inner_weight": inner_weight, "inner_bias": inner_bias, "outer_weight": outer_weight, "outer_bias": outer_bias, "norm2_gain": norm2_gain, "norm2_bias": norm2_bias, "output_grad": output_grad}


HIGH = lax.Precision.HIGHEST

@jax.custom_vjp
def low(v):
    return lax.optimization_barrier(v.astype(jnp.bfloat16)).astype(jnp.float32)

@jax.custom_vjp
def low_back(v):
    return v

def low_keep(v):
    return (low(v), None)

def low_pass(kept, grad):
    return (grad,)

def back_keep(v):
    return (v, None)

def back_low(kept, grad):
    return (low(grad),)
low.defvjp(low_keep, low_pass)
low_back.defvjp(back_keep, back_low)

def layer_norm(z, gain, shift):
    center = z - lax.optimization_barrier(jnp.mean(z, -1, keepdims=True))
    variance = lax.optimization_barrier(jnp.mean(center * center, -1, keepdims=True))
    return center * lax.rsqrt(variance + 1e-12) * gain + shift

def project(x, weight):
    return jnp.einsum('bsd,de->bse', x, weight, precision=HIGH)

def forward(params, x, segments, valid):
    query_weight, query_bias, key_weight, value_weight, value_bias, proj_weight, proj_bias, norm1_gain, norm1_bias, inner_weight, inner_bias, outer_weight, outer_bias, norm2_gain, norm2_bias = params
    nrows = x.shape[0]
    query = low(low_back(project(x, query_weight) + query_bias)).reshape(nrows, SEQ, HEADS, HD)
    keys = low(low_back(project(x, key_weight))).reshape(nrows, SEQ, HEADS, HD)
    values = low(low_back(project(x, value_weight) + value_bias)).reshape(nrows, SEQ, HEADS, HD)
    raw = jnp.einsum('bqhd,bkhd->bhqk', query, keys, precision=HIGH) * (1.0 / math.sqrt(HD))
    scores = low_back(raw)
    diagonal = jnp.eye(SEQ, dtype=jnp.int32) > 0
    allowed = (segments[:, :, None] == segments[:, None, :]) & ((valid[:, None, :] > 0) | diagonal[None])
    scores = jnp.where(allowed[:, None], scores, jnp.float32(-1000000000.0))
    top = lax.optimization_barrier(jnp.max(scores, -1, keepdims=True))
    expo = jnp.exp(scores - top)
    probs = expo / lax.optimization_barrier(jnp.sum(expo, -1, keepdims=True))
    context = jnp.einsum('bhqk,bkhd->bqhd', low(probs), values, precision=HIGH).reshape(nrows, SEQ, D)
    context = low(low_back(context))
    attn = low_back(project(context, proj_weight) + proj_bias)
    first = layer_norm(x + attn, norm1_gain, norm1_bias)
    pre = low_back(project(low(first), inner_weight) + inner_bias)
    inner = low(jax.nn.gelu(pre, approximate=False))
    ffn = low_back(project(inner, outer_weight) + outer_bias)
    return layer_norm(first + ffn, norm2_gain, norm2_bias)

def reference(hidden, segment_ids, pad_mask, query_weight, query_bias, key_weight, value_weight, value_bias, proj_weight, proj_bias, norm1_gain, norm1_bias, inner_weight, inner_bias, outer_weight, outer_bias, norm2_gain, norm2_bias, output_grad):
    params = tuple((p.astype(jnp.float32) for p in (query_weight, query_bias, key_weight, value_weight, value_bias, proj_weight, proj_bias, norm1_gain, norm1_bias, inner_weight, inner_bias, outer_weight, outer_bias, norm2_gain, norm2_bias)))
    block = math.gcd(ROWS, max(1, 4096 // SEQ))
    count = ROWS // block
    inputs = hidden.astype(jnp.float32).reshape(count, block, SEQ, D)
    cotangents = output_grad.astype(jnp.float32).reshape(count, block, SEQ, D)
    segments = segment_ids.astype(jnp.int32).reshape(count, block, SEQ)
    valid = pad_mask.astype(jnp.int32).reshape(count, block, SEQ)

    def step(totals, item):
        x_block, grad_block, seg_block, valid_block = item
        result, pull = jax.vjp(lambda p, xx: forward(p, xx, seg_block, valid_block), params, x_block)
        param_grads, x_grad = pull(grad_block)
        totals = jax.tree.map(lambda a, g: a + g, totals, param_grads)
        return (totals, (result, x_grad))
    zeros = jax.tree.map(jnp.zeros_like, params)
    grads, (results, x_grads) = lax.scan(step, zeros, (inputs, cotangents, segments, valid))
    output = results.reshape(TOKENS, D).astype(jnp.bfloat16)
    input_grad = x_grads.reshape(TOKENS, D)
    return (output, input_grad, grads[0], grads[1], grads[2], grads[3], grads[4], grads[5], grads[6], grads[7], grads[8], grads[9], grads[10], grads[11], grads[12], grads[13], grads[14])
```

```python
import math

import jax
import jax.numpy as jnp
from jax import lax
from jax.sharding import PartitionSpec as P

HD = 64
EPS = 1e-12
BF = jnp.bfloat16
F32 = jnp.float32


def norm_forward(z, gain, shift):
    center = z - jnp.mean(z, -1, keepdims=True)
    scale = lax.rsqrt(jnp.mean(center * center, -1, keepdims=True) + EPS)
    normed = center * scale
    return (normed * gain + shift, normed, scale)


def norm_backward(grad, normed, scale, gain):
    scaled = grad * gain
    first_mean = jnp.mean(scaled, -1, keepdims=True)
    second_mean = jnp.mean(scaled * normed, -1, keepdims=True)
    return scale * (scaled - first_mean - normed * second_mean)


def dot_tn(left, right):
    return lax.dot_general(left, right, (((0,), (0,)), ((), ())), preferred_element_type=F32)


def dot_nt(left, right):
    return lax.dot_general(left, right, (((1,), (1,)), ((), ())), preferred_element_type=F32)


def dot_nn(left, right):
    return jnp.dot(left, right, preferred_element_type=F32)


def allowed_pairs(seg_row, valid_row):
    size = seg_row.shape[0]
    diagonal = lax.broadcasted_iota(jnp.int32, (size, size), 0) == lax.broadcasted_iota(
        jnp.int32, (size, size), 1
    )
    same = seg_row[:, None] == seg_row[None, :]
    return same & ((valid_row[None, :] > 0) | diagonal)


def attend(q, k, v, keep):
    size, cols = q.shape
    heads = cols // HD
    factor = 1.0 / math.sqrt(HD)
    q4, k4, v4 = (t.reshape(size, heads, HD) for t in (q, k, v))
    raw = jnp.einsum("qhd,khd->hqk", q4, k4, preferred_element_type=F32) * factor
    scores = jnp.where(keep[None], raw, F32(-1000000000.0))
    top = jnp.max(scores, -1, keepdims=True)
    expo = jnp.exp(scores - top)
    total = jnp.sum(expo, -1, keepdims=True)
    probs = expo / total
    context = jnp.einsum("hqk,khd->qhd", probs.astype(BF), v4, preferred_element_type=F32)
    return context.astype(BF).reshape(size, cols), top + jnp.log(total)


def attend_back(q, k, v, g, log_total, keep):
    size, cols = q.shape
    heads = cols // HD
    factor = 1.0 / math.sqrt(HD)
    q4, k4, v4, g4 = (t.reshape(size, heads, HD) for t in (q, k, v, g))
    raw = jnp.einsum("qhd,khd->hqk", q4, k4, preferred_element_type=F32) * factor
    probs = jnp.where(keep[None], jnp.exp(raw - log_total), F32(0.0))
    dprobs = jnp.einsum("qhd,khd->hqk", g4, v4, preferred_element_type=F32)
    delta = jnp.sum(probs * dprobs, -1, keepdims=True)
    ds = (probs * (dprobs - delta)).astype(BF)
    dq = jnp.einsum("hqk,khd->qhd", ds, k4, preferred_element_type=F32) * factor
    dk = jnp.einsum("hqk,qhd->khd", ds, q4, preferred_element_type=F32) * factor
    dv = jnp.einsum("hqk,qhd->khd", probs.astype(BF), g4, preferred_element_type=F32)
    return tuple(t.astype(BF).reshape(size, cols) for t in (dq, dk, dv))


def swap(x, axis, bit, size):
    return lax.ppermute(x, axis, [(i, i ^ bit) for i in range(size)])


def plus(a, b):
    return (a.astype(F32) + b.astype(F32)).astype(BF)


def half(x, index, axis=0):
    size = x.shape[axis] // 2
    return lax.dynamic_slice_in_dim(x, index * size, size, axis)


def join(mine, other, index, axis=0):
    size = mine.shape[axis]
    out = jnp.concatenate([mine, mine], axis)
    return lax.dynamic_update_slice_in_dim(out, other, (1 - index) * size, axis)


def build(dp, mp):
    assert mp == 4 and dp & (dp - 1) == 0
    bits = [1 << i for i in range(dp.bit_length() - 1)]

    def fetch(first, second):
        own = (first, second)
        sib = tuple(swap(t, "mp", 1, mp) for t in own)
        got = swap(first, "mp", 2, mp)
        far = (got, swap(got, "dp", 1, dp))
        far_sib = tuple(swap(t, "mp", 1, mp) for t in far)
        return (own, sib, far, far_sib)

    def reduce_quarter(grads, place):
        got = [swap(t, "mp", 1, mp) for t in grads[1] + grads[3]]
        near = [plus(a, r) for a, r in zip(grads[0], got[:2])]
        far = [plus(a, r) for a, r in zip(grads[2], got[2:])]
        got = [swap(t, "mp", 2, mp) for t in far]
        near = [plus(a, r) for a, r in zip(near, got)]
        part = plus(near[0], swap(near[1], "dp", 1, dp))
        for bit in bits[1:]:
            index = (place // bit) % 2
            send = half(part, 1 - index)
            part = plus(half(part, index), swap(send, "dp", bit, dp))
        for bit in reversed(bits[1:]):
            index = (place // bit) % 2
            part = join(part, swap(part, "dp", bit, dp), index)
        return part, swap(part, "dp", 1, dp)

    def per_device(
        hidden, segment_ids, pad_mask, query_weight, query_bias, key_weight, value_weight,
        value_bias, proj_weight, proj_bias, norm1_gain, norm1_bias, inner_weight, inner_bias,
        outer_weight, outer_bias, norm2_gain, norm2_bias, output_grad,
    ):
        seq = segment_ids.shape[1]
        assert hidden.shape[0] == seq
        heads_cols = query_weight.shape[1]
        place = lax.axis_index("dp")
        me = lax.axis_index("mp")
        b = place % 2
        seg = lax.dynamic_index_in_dim(segment_ids, me, 0, keepdims=False)
        valid = lax.dynamic_index_in_dim(pad_mask, me, 0, keepdims=False)
        keep = allowed_pairs(seg, valid)

        pack = jnp.concatenate([query_weight.T, key_weight.T, value_weight.T, proj_weight], 0)
        att = fetch(half(pack, b), half(pack, 1 - b))
        att = [join(*t, b) for t in att]
        w1 = fetch(half(inner_weight, b, 1), half(inner_weight, 1 - b, 1))
        w2 = fetch(half(outer_weight, b), half(outer_weight, 1 - b))
        tiny = jnp.concatenate(
            [query_bias, value_bias, half(inner_bias, b), half(inner_bias, 1 - b)]
        )
        tiny = [tiny, swap(tiny, "mp", 1, mp)]
        tiny = tiny + [swap(t, "mp", 2, mp) for t in tiny]
        n = heads_cols
        tiny = [t.astype(F32) for t in tiny]
        bq, bv, b1 = ([t[s] for t in tiny] for s in (slice(0, n), slice(n, 2 * n), slice(2 * n, None)))

        q, k, v, wo = [], [], [], []
        for j in range(4):
            wq_t, wk_t, wv_t, w_o = (att[j][i * n : (i + 1) * n] for i in range(4))
            q.append((dot_nt(hidden, wq_t) + bq[j]).astype(BF))
            k.append(dot_nt(hidden, wk_t).astype(BF))
            v.append((dot_nt(hidden, wv_t) + bv[j]).astype(BF))
            wo.append(w_o)
        attn = 0.0
        context, log_total = [], []
        for j in range(4):
            c, l = attend(q[j], k[j], v[j], keep)
            context.append(c)
            log_total.append(l)
            attn = attn + dot_nn(c, wo[j])
        gain_one = norm1_gain.astype(F32)
        gain_two = norm2_gain.astype(F32)
        first, normed_one, scale_one = norm_forward(
            hidden.astype(F32) + attn + proj_bias.astype(F32), gain_one, norm1_bias.astype(F32)
        )
        low = first.astype(BF)
        ffn = 0.0
        pre, inner = [], []
        units = w2[0][0].shape[0]
        for j in range(4):
            for h in range(2):
                p = dot_nn(low, w1[j][h]) + b1[j][h * units : (h + 1) * units]
                i = jax.nn.gelu(p, approximate=False).astype(BF)
                pre.append(p)
                inner.append(i)
                ffn = ffn + dot_nn(i, w2[j][h])
        second, normed_two, scale_two = norm_forward(
            first + ffn + outer_bias.astype(F32), gain_two, norm2_bias.astype(F32)
        )
        cot = output_grad.astype(F32)
        norm2_gain_grad = jnp.sum(cot * normed_two, 0)
        norm2_bias_grad = jnp.sum(cot, 0)
        second_grad = norm_backward(cot, normed_two, scale_two, gain_two)
        dffn = second_grad.astype(BF)
        outer_bias_grad = jnp.sum(dffn.astype(F32), 0)

        g2 = [[dot_tn(inner[2 * j + h], dffn).astype(BF) for h in range(2)] for j in range(4)]
        w2_grad = reduce_quarter([tuple(t) for t in g2], place)
        first_grad = second_grad
        g1, g_b1 = [], []
        for j in range(4):
            pair, pair_b = [], []
            for h in range(2):
                p = pre[2 * j + h]
                _, pull = jax.vjp(lambda t: jax.nn.gelu(t, approximate=False), p)
                dpre = pull(dot_nt(dffn, w2[j][h]))[0].astype(BF)
                first_grad = first_grad + dot_nt(dpre, w1[j][h])
                pair.append(dot_tn(dpre, low).astype(BF))
                pair_b.append(jnp.sum(dpre.astype(F32), 0))
            g1.append(tuple(pair))
            g_b1.append(jnp.concatenate(pair_b))
        w1_grad = reduce_quarter(g1, place)
        norm1_gain_grad = jnp.sum(first_grad * normed_one, 0)
        norm1_bias_grad = jnp.sum(first_grad, 0)
        attn_grad_full = norm_backward(first_grad, normed_one, scale_one, gain_one)
        dattn = attn_grad_full.astype(BF)
        proj_bias_grad = jnp.sum(dattn.astype(F32), 0)
        input_grad = attn_grad_full
        ga, g_bq, g_bv = [], [], []
        for j in range(4):
            wq_t, wk_t, wv_t = (att[j][i * n : (i + 1) * n] for i in range(3))
            dctx = dot_nt(dattn, wo[j]).astype(BF)
            dq, dk, dv = attend_back(q[j], k[j], v[j], dctx, log_total[j], keep)
            input_grad = input_grad + dot_nn(dq, wq_t) + dot_nn(dk, wk_t) + dot_nn(dv, wv_t)
            g = jnp.concatenate(
                [dot_tn(t, hidden).astype(BF) for t in (dq, dk, dv)]
                + [dot_tn(context[j], dattn).astype(BF)], 0,
            )
            ga.append((half(g, b), half(g, 1 - b)))
            g_bq.append(jnp.sum(dq.astype(F32), 0))
            g_bv.append(jnp.sum(dv.astype(F32), 0))
        att_grad = join(*reduce_quarter(ga, place), b).astype(F32)

        wide = jnp.stack(
            [proj_bias_grad, norm1_gain_grad, norm1_bias_grad, outer_bias_grad, norm2_gain_grad, norm2_bias_grad]
        )
        rel = jnp.stack([jnp.concatenate([g_bq[j], g_bv[j], g_b1[j]]) for j in range(4)])
        for bit in (1, 2):
            got_w, got_r = swap(wide, "mp", bit, mp), swap(rel, "mp", bit, mp)
            wide = wide + got_w
            rel = rel + jnp.stack([got_r[j ^ bit] for j in range(4)])
        rel = rel[0]
        for bit in bits:
            got_w, got_r = swap(wide, "dp", bit, dp), swap(rel, "dp", bit, dp)
            wide = wide + got_w
            if bit == 1:
                got_r = jnp.concatenate([got_r[: 2 * n], got_r[2 * n + units :], got_r[2 * n : 2 * n + units]])
            rel = rel + got_r
        b1_grad = join(rel[2 * n : 2 * n + units], rel[2 * n + units :], b)
        return (
            second.astype(BF),
            input_grad,
            att_grad[:n].T,
            rel[:n],
            att_grad[n : 2 * n].T,
            att_grad[2 * n : 3 * n].T,
            rel[n : 2 * n],
            att_grad[3 * n :],
            wide[0],
            wide[1],
            wide[2],
            join(*w1_grad, b).astype(F32).T,
            b1_grad,
            join(*w2_grad, b).astype(F32),
            wide[3],
            wide[4],
            wide[5],
        )

    return per_device


def solution(mesh):
    rows, cols, rep = P(("dp", "mp"), None), P(None, "mp"), P()
    vec, up = P("mp"), P("mp", None)
    return jax.shard_map(
        build(mesh.shape["dp"], mesh.shape["mp"]),
        mesh=mesh,
        in_specs=(
            rows, P("dp", None), P("dp", None), cols, vec, cols, cols, vec, up, rep,
            rep, rep, cols, vec, up, rep, rep, rep, rows,
        ),
        out_specs=(
            rows, rows, cols, vec, cols, cols, vec, up, rep, rep, rep, cols, vec, up, rep, rep, rep,
        ),
        check_vma=False,
    )
```

```python
import functools
import math

import jax
import jax.numpy as jnp
from jax import lax
from jax.experimental import pallas as pl
from jax.experimental.pallas import tpu as pltpu
from jax.sharding import PartitionSpec as P


HD = 64
MOST = 64
QB = 128
WIN = QB + 2 * MOST
TILE = 16
EPS = 1e-12
BF = jnp.bfloat16
F32 = jnp.float32
SMEM = pltpu.SMEM
VMEM = pltpu.VMEM


def dot_nn(left, right):
    return lax.dot_general(left, right, (((1,), (0,)), ((), ())), preferred_element_type=F32)


def dot_nt(left, right):
    return lax.dot_general(left, right, (((1,), (1,)), ((), ())), preferred_element_type=F32)


def dot_tn(left, right):
    return lax.dot_general(left, right, (((0,), (0,)), ((), ())), preferred_element_type=F32)


def shape(dims, kind):
    return jax.ShapeDtypeStruct(dims, kind)


def call(body, outs, ins, scratch=(), smem=0, any_at=(), plain=(), far=(), flush=(), us=10.0, mib=10):
    def spec(i):
        if i < smem:
            return pl.BlockSpec(memory_space=SMEM)
        if i in any_at:
            return pl.BlockSpec(memory_space=pltpu.HBM)
        return pl.BlockSpec(memory_space=VMEM)

    held = [(pltpu.HBM if i in far or i in flush else VMEM)(o.shape, o.dtype) for i, o in enumerate(outs)]
    ins = [
        x if i < smem else pltpu.with_memory_space_constraint(x, pltpu.HBM if i in plain or i in any_at else VMEM)
        for i, x in enumerate(ins)
    ]
    return pl.pallas_call(
        body,
        out_shape=tuple(held),
        in_specs=[spec(i) for i in range(len(ins))],
        out_specs=tuple(pl.BlockSpec(memory_space=pltpu.HBM if i in far else VMEM) for i in range(len(outs))),
        scratch_shapes=list(scratch),
        compiler_params=pltpu.CompilerParams(vmem_limit_bytes=mib << 20),
        cost_estimate=pl.CostEstimate(flops=int(us * 1e9), transcendentals=0, bytes_accessed=0),
    )(*ins)


def pack_body(
    scal, wq, wk, wv, wo, w1, w2, bq, bv, b1, pb, g1, s1, ob, g2, s2,
    own, lead, rest, w1_lead, w1_rest, w2_lead, w2_rest, small, own_far, sem,
):
    b = scal[0]
    n = wq.shape[0]
    third = lead.shape[0]
    units = w2_lead.shape[0]
    first = pl.multiple_of(b * units, units)
    small[...] = jnp.zeros_like(small)
    small[0, :n] = bq[...].astype(F32)
    small[0, 2 * n : 3 * n] = bv[...].astype(F32)
    for i, ref in enumerate((b1, pb, g1, s1, ob, g2, s2)):
        small[i + 1, :] = ref[...].astype(F32)
    for i, ref in enumerate((wq, wk, wv, wo)):
        own[i * n : (i + 1) * n, :] = ref[...]
    row = small[1:2, :]
    turned = jnp.concatenate([row[:, units : 2 * units], row[:, :units], row[:, 2 * units :]], 1)
    own[4 * n :, :] = jnp.concatenate(
        [small[0:1, :], jnp.where(b == 0, row, turned), row, jnp.zeros((TILE - 3, small.shape[1]), F32)], 0
    ).astype(BF)
    far = pltpu.make_async_copy(own, own_far, sem.at[0])
    far.start()
    lead[...] = own[pl.ds(pl.multiple_of(b * third, third), third), :]
    rest[...] = own[2 * third :, :]
    w1_lead[...] = w1[:, pl.ds(first, units)]
    w2_lead[...] = w2[pl.ds(first, units), :]
    w1_rest[...] = w1[:, 2 * units :]
    w2_rest[...] = w2[2 * units :, :]
    far.wait()


def prepare(scal, seg_ref, pad_ref, hidden, hid, code):
    size = hidden.shape[0]
    me = scal[1]
    zero = jnp.zeros((MOST, hidden.shape[1]), BF)
    hid[:MOST, :] = zero
    hid[MOST : MOST + size, :] = hidden[...]
    hid[MOST + size :, :] = zero
    seg = seg_ref[pl.ds(me, 1), :].astype(F32)
    valid = pad_ref[pl.ds(me, 1), :]
    keys = jnp.where(valid > 0, seg, -1.0)
    empty = jnp.full((MOST, QB), -1.0, F32)
    code[:MOST, :] = empty
    code[MOST : MOST + size, :] = jnp.transpose(jnp.broadcast_to(keys, (QB, size)))
    code[MOST + size :, :] = empty
    return seg


def block_masks(seg, code, masks):
    diagonal = lax.broadcasted_iota(jnp.int32, (WIN, QB), 0) == MOST + lax.broadcasted_iota(
        jnp.int32, (WIN, QB), 1
    )
    for i in range(masks.shape[0]):
        same = code[i * QB : i * QB + WIN, :] == seg[:, i * QB : (i + 1) * QB]
        masks[i] = jnp.where(same | diagonal, 1.0, 0.0)


def column(row):
    return jnp.transpose(jnp.broadcast_to(row, (QB, row.shape[1])))


def bias_column(pack_tail, start, n):
    wide = -(-(start + n) // QB) * QB
    return column(pack_tail[0:1, :wide].astype(F32))[start : start + n]


def saved_scratch(n, size, pads, heads):
    return [
        VMEM((n, size), BF), VMEM((2 * n, pads), BF), VMEM((n, size), BF), VMEM((heads, 1, size), F32),
        pltpu.SemaphoreType.DMA((8,)),
    ]


def attend_quarter(w, tail, hidden, hid, masks, saved, work, ktok):
    qt, kvt, ctxt, lse, sems = work
    copies = [pltpu.make_async_copy(src, dst, sems.at[i]) for i, (src, dst) in enumerate(zip(work[:4], saved))]
    size = hidden.shape[0]
    n = w.shape[0] // 4
    reps = size // QB
    bq = bias_column(tail, 0, n)
    bv = bias_column(tail, 2 * n, n)
    q = dot_nt(w[0:n, :], hidden[...])
    qt[...] = ((q + jnp.concatenate([bq] * reps, 1)).astype(BF).astype(F32) * (1.0 / math.sqrt(HD))).astype(BF)
    kvt[:n, :] = dot_nt(w[n : 2 * n, :], hid[...]).astype(BF)
    kvt[n:, :] = (dot_nt(w[2 * n : 3 * n, :], hid[...]) + jnp.concatenate([bv] * (reps + 1), 1)).astype(BF)
    copies[0].start()
    copies[1].start()

    def head(h, carry):
        at = pl.multiple_of(h * HD, HD)
        ktok[...] = jnp.transpose(kvt[pl.ds(at, HD), :])
        for i in range(reps):
            lanes = slice(i * QB, (i + 1) * QB)
            keys = slice(i * QB, i * QB + WIN)
            s = dot_nn(ktok[keys, :], qt[pl.ds(at, HD), lanes])
            s = jnp.where(masks[i] > 0.0, s, F32(-1000000000.0))
            top = jnp.max(s, 0, keepdims=True)
            e = jnp.exp(s - top)
            total = jnp.sum(e, 0, keepdims=True)
            p = (e * (1.0 / total)).astype(BF)
            ctxt[pl.ds(at, HD), lanes] = dot_nn(kvt[pl.ds(n + at, HD), keys], p).astype(BF)
            lse[h, :, lanes] = top + jnp.log(total)
        return carry

    lax.fori_loop(0, n // HD, head, 0)
    copies[2].start()
    copies[3].start()
    return dot_tn(ctxt[...], w[3 * n : 4 * n, :]), copies


def near_attention(scal, seg_ref, pad_ref, hidden, pack, *refs):
    before, refs = refs[:-15], refs[-15:]
    saved, (acc, b1), (hid, code, masks, ktok), work = refs[:4], refs[4:6], refs[6:10], refs[10:]
    seg = prepare(scal, seg_ref, pad_ref, hidden, hid, code)
    block_masks(seg, code, masks)
    n = pack.shape[0] // 4 // TILE * TILE
    tail = pack.at[4 * n :]
    spread_bias(tail, 2, b1)
    part, copies = attend_quarter(pack.at[: 4 * n], tail, hidden, hid, masks, saved, work, ktok)
    acc[...] = part + before[0][...] if before else part
    for c in copies:
        c.wait()


def spread_bias(tail, row, out):
    units = out.shape[2]
    for k in range(out.shape[0]):
        out[k] = tail[row : row + 1, k * units : (k + 1) * units].astype(F32)


def order(b, lead, other, rest, out):
    size = lead.shape[0]
    out[pl.ds(pl.multiple_of(b * size, size), size), :] = lead[...]
    out[pl.ds(pl.multiple_of((1 - b) * size, size), size), :] = other[...]
    out[2 * size :, :] = rest[: out.shape[0] - 2 * size, :]


def stats(z):
    center = z - jnp.mean(z, -1, keepdims=True)
    scale = lax.rsqrt(jnp.mean(center * center, -1, keepdims=True) + EPS)
    return center * scale, scale


def far_attention(scal, seg_ref, pad_ref, hidden, lead, other, rest, before, *refs, last):
    small = refs[0] if last else None
    refs = refs[1:] if last else refs
    saved, (pack_out, b1), more = refs[:4], refs[4:6], refs[6:-10]
    pack, hid, code, masks, ktok = refs[-10:-5]
    work = refs[-5:]
    seg = prepare(scal, seg_ref, pad_ref, hidden, hid, code)
    block_masks(seg, code, masks)
    order(scal[0], lead, other, rest, pack)
    sems = work[4]
    outs = [pltpu.make_async_copy(pack, pack_out, sems.at[4])]
    outs[0].start()
    tail = rest.at[rest.shape[0] - TILE :]
    spread_bias(tail, 1, b1)
    part, copies = attend_quarter(pack, tail, hidden, hid, masks, saved, work, ktok)
    outs += copies
    total = before[...] + part
    if last:
        first, low, normed, scale = more
        normed[...] = total

        def norm(i, carry):
            at = pl.ds(pl.multiple_of(i * STEP, STEP), STEP)
            unit, r = stats(hidden[at, :].astype(F32) + normed[at, :] + small[2:3, :])
            h1 = unit * small[3:4, :] + small[4:5, :]
            first[at, :] = h1
            low[at, :] = h1.astype(BF)
            normed[at, :] = unit
            scale[at, :] = jnp.broadcast_to(r, (STEP, scale.shape[1]))
            return carry

        lax.fori_loop(0, hidden.shape[0] // STEP, norm, 0)
    else:
        more[0][...] = total
    for c in outs:
        c.wait()


def attention_back(
    scal, seg_ref, pad_ref, hidden, dattn, grad, rows1, rows2, gb, pack, qt, kvt, ctxt, lse,
    upper, lower, acc, hid, code, masks, ktok, vtok, dqkv, dk, dv, dctx, tile,
):
    size = hidden.shape[0]
    reps = size // QB
    seg = prepare(scal, seg_ref, pad_ref, hidden, hid, code)
    block_masks(seg, code, masks)
    n = pack.shape[0] // 4 // TILE * TILE
    dctx[...] = dot_nt(pack[3 * n : 4 * n, :], dattn[...]).astype(BF)
    lower[n:, :] = dot_nn(ctxt[...], dattn[...]).astype(BF)

    def head(h, carry):
        at = pl.multiple_of(h * HD, HD)
        ktok[...] = jnp.transpose(kvt[pl.ds(at, HD), :])
        vtok[...] = jnp.transpose(kvt[pl.ds(n + at, HD), :])
        dk[...] = jnp.zeros_like(dk)
        dv[...] = jnp.zeros_like(dv)
        for i in range(reps):
            lanes = slice(i * QB, (i + 1) * QB)
            keys = slice(i * QB, i * QB + WIN)
            q = qt[pl.ds(at, HD), lanes]
            g = dctx[pl.ds(at, HD), lanes]
            s = dot_nn(ktok[keys, :], q)
            p = jnp.where(masks[i] > 0.0, jnp.exp(s - lse[h, :, lanes]), 0.0)
            dp = dot_nn(vtok[keys, :], g)
            delta = jnp.sum(p * dp, 0, keepdims=True)
            ds = (p * (dp - delta)).astype(BF)
            dq = dot_nn(kvt[pl.ds(at, HD), keys], ds) * (1.0 / math.sqrt(HD))
            dqkv[pl.ds(at, HD), lanes] = dq.astype(BF)
            dk[:, keys] += dot_nt(q, ds)
            dv[:, keys] += dot_nt(g, p.astype(BF))
        wide = dk.shape[1]
        dqkv[pl.ds(n + at, HD), :] = pltpu.roll(dk[...], wide - MOST, 1)[:, :size].astype(BF)
        dqkv[pl.ds(2 * n + at, HD), :] = pltpu.roll(dv[...], wide - MOST, 1)[:, :size].astype(BF)
        return carry

    lax.fori_loop(0, n // HD, head, 0)
    upper[: 2 * n, :] = dot_nn(dqkv[: 2 * n, :], hidden[...]).astype(BF)
    lower[:n, :] = dot_nn(dqkv[2 * n :, :], hidden[...]).astype(BF)
    acc[...] = grad[...] + dot_tn(dqkv[...], pack[: 3 * n, :])
    bias = dot_nt(jnp.ones((8, size), BF), dqkv[...])
    units = gb.shape[2]
    tile[...] = jnp.zeros_like(tile)
    tile[0:1, :n] = bias[0:1, :n]
    tile[0:1, 2 * n : 3 * n] = bias[0:1, 2 * n :]
    for k in range(gb.shape[0]):
        tile[1:2, k * units : (k + 1) * units] = gb[k]
    tile[2:5, :] = rows1[0:3, :]
    tile[5:8, :] = rows2[0:3, :]
    upper[2 * n :, :] = jnp.zeros((upper.shape[0] - 2 * n, upper.shape[1]), BF)
    upper[2 * n : 2 * n + TILE, :] = tile[...].astype(BF)


TAIL = (
    0.11762539007438957, 0.046694333975460314, 0.3222211738117182, -0.31396123834780804, 0.440880529781562,
    -0.11346019315654339,
)
TAIL_P = 0.27599385522864645


def gelu_pair(x):
    t = 1.0 / (1.0 + TAIL_P * jnp.abs(x))
    e = jnp.exp2((x * x) * (-0.5 / math.log(2.0)))
    g = F32(TAIL[-1])
    for c in TAIL[-2::-1]:
        g = g * t + c
    g = g * (t * e)
    phi = jnp.where(x >= 0.0, 1.0 - g, g)
    return x * phi, phi + x * (e * (1.0 / math.sqrt(2.0 * math.pi)))


def quarter_copies(w1, w2, b1, b2, sems):
    if len(w1) == 1:
        parts = [(w1[0], b1), (w2[0], b2)]
    else:
        u = b2.shape[0] // 3
        parts = [(w, b1.at[:, k * u : (k + 1) * u]) for k, w in enumerate(w1)]
        parts += [(w, b2.at[k * u : (k + 1) * u, :]) for k, w in enumerate(w2)]
    copies = [pltpu.make_async_copy(src, dst, sems.at[i]) for i, (src, dst) in enumerate(parts)]
    n = len(w1)
    return copies[:n], copies[n:]


ROWS = 256


def ffn_scratch(size, width, units):
    return [
        VMEM((2, width, 3 * units), BF), VMEM((2, 3 * units, width), BF), VMEM((2, size, 3 * units), BF),
        VMEM((2, size, 3 * units), BF), VMEM((2, 8, 3 * units), F32), pltpu.SemaphoreType.DMA((2, 6)),
        pltpu.SemaphoreType.DMA((4,)),
    ]


def inner_scratch(size, width, units):
    return [
        VMEM((width, size), BF), VMEM((size, 3 * units), BF), VMEM((2, width, 3 * units), BF),
        VMEM((2, 3 * units, width), BF), VMEM((2, size, 3 * units), BF), VMEM((2, width, 3 * units), BF),
        VMEM((2, 3, 1, units), F32), pltpu.SemaphoreType.DMA((2, 7)),
    ]


def ffn_pair(weights, biases, low, start, acc, inner, slope, w1_buf, w2_buf, in_buf, sl_buf, bias_buf, sems, out_sems):
    copies = [
        quarter_copies(w1, w2, w1_buf.at[j], w2_buf.at[j], sems.at[j]) for j, (w1, w2) in enumerate(weights)
    ]
    for first, second in copies:
        for c in first + second:
            c.start()
    both = biases[0].shape[0]
    for k in range(both):
        for j, b1 in enumerate(biases):
            u = b1.shape[2]
            bias_buf[j, 0:1, k * u : (k + 1) * u] = b1[k]
    acc[...] = jnp.zeros_like(acc) if start is None else start[...]
    n = len(copies[0][0])

    def waits(j, at, dst):
        u = dst.shape[2] // 3 if at == 0 else dst.shape[1] // 3
        for k in range(n):
            if n == 1:
                part = dst.at[j]
            else:
                part = dst.at[j, :, k * u : (k + 1) * u] if at == 0 else dst.at[j, k * u : (k + 1) * u, :]
            pltpu.make_async_copy(part, part, sems.at[j, at * n + k]).wait()

    def quarter(j, carry):
        waits(j, 0, w1_buf)
        for r in range(0, low.shape[0], ROWS):
            rows = slice(r, r + ROWS)
            act, der = gelu_pair(dot_nn(low[rows, :], w1_buf[j]) + bias_buf[j, 0:1, :])
            in_buf[j, rows, :] = act.astype(BF)
            sl_buf[j, rows, :] = der.astype(BF)
        waits(j, 1, w2_buf)
        for i, (buf, out) in enumerate(((in_buf, inner), (sl_buf, slope))):
            pltpu.make_async_copy(buf.at[j], out.at[j], out_sems.at[2 * j + i]).start()
        for r in range(0, low.shape[0], ROWS):
            rows = slice(r, r + ROWS)
            acc[rows, :] += dot_nn(in_buf[j, rows, :], w2_buf[j])
        return carry

    lax.fori_loop(0, 2, quarter, 0)
    return [
        pltpu.make_async_copy(buf.at[j], out.at[j], out_sems.at[2 * j + i])
        for j in range(2)
        for i, (buf, out) in enumerate(((in_buf, inner), (sl_buf, slope)))
    ]


def near_ffn(low, w1a, w1b, w2a, w2b, b1_a, b1_b, inner, slope, acc, *scratch):
    outs = ffn_pair([((w1a,), (w2a,)), ((w1b,), (w2b,))], (b1_a, b1_b), low, None, acc, inner, slope, *scratch)
    for c in outs:
        c.wait()


def norm_back(grad, unit, r, gain):
    scaled = grad * gain
    m1 = jnp.mean(scaled, -1, keepdims=True)
    m2 = jnp.mean(scaled * unit, -1, keepdims=True)
    return r * (scaled - m1 - unit * m2)


def row_sums(rows, at, *terms):
    for i, t in enumerate(terms):
        total = jnp.sum(t, 0, keepdims=True)
        rows[i : i + 1, :] = total if at == 0 else rows[i : i + 1, :] + total


STEP = 256


def far_ffn(
    w1a0, w1a1, w1a2, w1b0, w1b1, w1b2, w2a0, w2a1, w2a2, w2b0, w2b1, w2b2, low, b1_a, b1_b, near, first, cot, small,
    inner, slope, out, dz, dffn, rows, acc, *scratch,
):
    outs = ffn_pair(
        [((w1a0, w1a1, w1a2), (w2a0, w2a1, w2a2)), ((w1b0, w1b1, w1b2), (w2b0, w2b1, w2b2))], (b1_a, b1_b), low, near,
        acc, inner, slope, *scratch,
    )
    rows[...] = jnp.zeros_like(rows)

    def norm(i, carry):
        at = pl.ds(pl.multiple_of(i * STEP, STEP), STEP)
        unit, r = stats(first[at, :] + acc[at, :] + small[5:6, :])
        out[at, :] = (unit * small[6:7, :] + small[7:8, :]).astype(BF)
        g = cot[at, :].astype(F32)
        d = norm_back(g, unit, r, small[6:7, :])
        dz[at, :] = d
        d = d.astype(BF)
        dffn[at, :] = d
        row_sums(rows, 1, d.astype(F32), g * unit, g)
        return carry

    lax.fori_loop(0, low.shape[0] // STEP, norm, 0)
    for c in outs:
        c.wait()


def spots(b, far):
    return [b, 1 - b, 2] if far else [0, 1, 2]


def third(k, u):
    return pl.ds(pl.multiple_of(k * u, u), u)


def outer_back(scal, acts, dffn, *refs, index, far):
    outs, (buf, sems) = refs[:-2], refs[-2:]
    copies = [pltpu.make_async_copy(acts.at[k], buf.at[i], sems.at[i]) for i, k in enumerate(index)]
    for c in copies:
        c.start()
    u = outs[0].shape[0] // 3

    def quarter(j, carry):
        pltpu.make_async_copy(buf.at[j], buf.at[j], sems.at[j]).wait()
        grad = dot_tn(buf[j], dffn[...]).astype(BF)
        buf_out = outs[0] if len(outs) == 1 else None
        if buf_out is not None:
            for k, spot in enumerate(spots(scal[0], far)):
                buf_out[third(spot, u), :] = grad[k * u : (k + 1) * u, :]
        else:
            for i, out in enumerate(outs):

                @pl.when(j == i)
                def _(out=out):
                    out[...] = grad

        return carry

    lax.fori_loop(0, len(index), quarter, 0)


def inner_pair(
    scal, weights, far, slope, low, dffn, start, sent, kept, gb_s, gb_k, acc, low_t, dpre, w1_buf, w2_buf, sl_buf, both, gb_both, sems,
):
    copies = []
    for j, (w1, w2) in enumerate(weights):
        first, second = quarter_copies(w1, w2, w1_buf.at[j], w2_buf.at[j], sems.at[j])
        copies.append((second + [pltpu.make_async_copy(slope.at[1 - j], sl_buf.at[j], sems.at[j, 6])], first))
        for c in copies[j][0] + first:
            c.start()
    low_t[...] = jnp.transpose(low[...])
    acc[...] = start[...]
    n = len(weights[0][0])
    place = spots(scal[0], far)
    u = sent.shape[1] // 3

    def waits(j, at, dst):
        for k in range(n):
            if n == 1:
                part = dst.at[j]
            else:
                part = dst.at[j, :, k * u : (k + 1) * u] if at == 0 else dst.at[j, k * u : (k + 1) * u, :]
            pltpu.make_async_copy(part, part, sems.at[j, at * n + k]).wait()

    def quarter(j, carry):
        waits(j, 1, w2_buf)
        pltpu.make_async_copy(slope.at[0], sl_buf.at[j], sems.at[j, 6]).wait()
        d = (dot_nt(dffn[...], w2_buf[j]) * sl_buf[j].astype(F32)).astype(BF)
        dpre[...] = d
        grad = dot_nn(low_t[...], dpre[...]).astype(BF)
        bias = jnp.sum(d.astype(F32), 0, keepdims=True)
        for k, spot in enumerate(place):
            both[j, :, third(spot, u)] = grad[:, k * u : (k + 1) * u]
            gb_both[j, spot] = bias[:, k * u : (k + 1) * u]
        waits(j, 0, w1_buf)
        acc[...] += dot_nt(dpre[...], w1_buf[j])
        return carry

    lax.fori_loop(0, 2, quarter, 0)
    sent[...] = both[0]
    kept[...] = both[1]
    gb_s[...] = gb_both[0]
    gb_k[...] = gb_both[1]


def inner_far(
    scal, w1a0, w1a1, w1a2, w1b0, w1b1, w1b2, w2a0, w2a1, w2a2, w2b0, w2b1, w2b2, slope, low, dffn, dz,
    sent, kept, gb_s, gb_k, acc, *scratch,
):
    weights = [((w1b0, w1b1, w1b2), (w2b0, w2b1, w2b2)), ((w1a0, w1a1, w1a2), (w2a0, w2a1, w2a2))]
    inner_pair(scal, weights, True, slope, low, dffn, dz, sent, kept, gb_s, gb_k, acc, *scratch)


def inner_near(
    scal, w1a, w1b, w2a, w2b, slope, normed_far, scale_far, low, dffn, dz, small,
    sent, kept, gb_s, gb_k, dz1, dattn, rows, acc, normed, scale, norm_sems, *scratch,
):
    copies = [
        pltpu.make_async_copy(normed_far, normed, norm_sems.at[0]), pltpu.make_async_copy(scale_far, scale, norm_sems.at[1])
    ]
    for c in copies:
        c.start()
    weights = [((w1b,), (w2b,)), ((w1a,), (w2a,))]
    inner_pair(scal, weights, False, slope, low, dffn, dz, sent, kept, gb_s, gb_k, acc, *scratch)
    for c in copies:
        c.wait()
    rows[...] = jnp.zeros_like(rows)

    def norm(i, carry):
        at = pl.ds(pl.multiple_of(i * STEP, STEP), STEP)
        grad = acc[at, :]
        unit = normed[at, :]
        d = norm_back(grad, unit, scale[at, 0:1], small[3:4, :])
        dz1[at, :] = d
        d = d.astype(BF)
        dattn[at, :] = d
        row_sums(rows, 1, d.astype(F32), grad * unit, grad)
        return carry

    lax.fori_loop(0, low.shape[0] // STEP, norm, 0)


def swap(x, axis, bit, size):
    return lax.ppermute(x, axis, [(i, i ^ bit) for i in range(size)])


def total(terms):
    return sum(t.astype(F32) for t in terms).astype(BF)


def half(x, index):
    size = x.shape[0] // 2
    return lax.dynamic_slice_in_dim(x, index * size, size, 0)


def joined(mine, other, index):
    twice = jnp.concatenate([mine, mine], 0)
    return lax.dynamic_update_slice_in_dim(twice, other, (1 - index) * mine.shape[0], 0)


def rows_at(i, size):
    return pl.ds(pl.multiple_of(i * size, size), size)


def near_body(scal, x, y, z, out):
    rows = rows_at(1 - scal[0], out.shape[0])
    out[...] = total([x[rows, :], y[rows, :], z[...]])


def first_body(scal, x, y, z, w, keep, send, *, at):
    size = keep.shape[0]
    for out, i in ((keep, scal[at]), (send, 1 - scal[at])):
        wide, rows = rows_at(2 * scal[0] + i, size), rows_at(i, size)
        out[...] = total([x[wide, :], y[wide, :], z[rows, :], w[rows, :]])


def next_body(scal, *refs, at):
    terms, (keep, send) = refs[:-2], refs[-2:]
    size = keep.shape[0]
    for out, i in ((keep, scal[at]), (send, 1 - scal[at])):
        out[...] = total([t[rows_at(i, size), :] for t in terms])


def sum_body(scal, *refs):
    refs[-1][...] = total([t[...] for t in refs[:-1]])


def join_body(scal, mine, other, *outs, at):
    size = mine.shape[0]
    i = scal[at]
    if len(outs) == 2:
        for out, ref in zip(outs, (i, 1 - i)):
            out[...] = jnp.where(ref == 0, mine[...].astype(F32), other[...].astype(F32))
    else:
        out = outs[0]
        out[rows_at(i, size), :] = mine[...].astype(out.dtype)
        out[rows_at(1 - i, size), :] = other[...].astype(out.dtype)


def upper_body(scal, mine, other, q, k, vec):
    n, size = q.shape[0], mine.shape[0]
    mine, other = mine[...].astype(F32), other[...].astype(F32)
    first = scal[2] == 0
    low, high = jnp.where(first, mine, other), jnp.where(first, other, mine)
    both = [(low, 0), (high, size)]
    for out, start in ((q, 0), (k, n), (vec, 2 * n)):
        for ref, at in both:
            a, z = max(start, at), min(start + out.shape[0], at + size)
            if a < z:
                out[a - start : z - start, :] = ref[a - at : z - at, :]


def build(dp, mp):
    assert mp == 4 and dp & (dp - 1) == 0
    bits = [1 << i for i in range(dp.bit_length() - 1)]

    def over_mp(x, bit):
        return swap(x, "mp", bit, mp)

    def over_dp(x, bit):
        return swap(x, "dp", bit, dp)

    def reduce_quarters(far_sent, far_kept, near_sent, near_kept, scal, outs):
        width = far_kept.shape[1]

        def run(body, rows, ins, plain, kinds=(BF,), **more):
            if rows % TILE:
                return plain()
            outs = tuple(shape((rows, width), kind) for kind in kinds)
            return call(body, outs, ins, smem=1, us=1.0, mib=6, **more)

        def halves(x, i):
            return half(x, scal[i]), half(x, 1 - scal[i])

        def split(terms, i):
            return run(
                functools.partial(next_body, at=i), terms[0].shape[0] // 2, (scal, *terms),
                lambda: halves(total(terms), i), (BF, BF),
            )

        size = far_kept.shape[0]
        far = (far_kept, over_mp(far_sent, 1))
        ours = (near_kept, over_mp(near_sent, 1))
        keep, send = split(far, 2)
        xb = over_mp(send, 2)
        xa = over_mp(keep, 2)
        plain = [half(t, 1 - scal[0]) for t in ours] + [xb]
        (send,) = run(near_body, size // 2, (scal, *ours, xb), lambda: (total(plain),))
        y = over_dp(send, 1)
        terms = ours + (xa, y)
        for i in range(1, len(bits)):
            if len(terms) == 4:
                wide = [half(t, scal[0]) for t in terms[:2]] + list(terms[2:])
                keep, send = run(
                    functools.partial(first_body, at=2 + i), size // 4, (scal, *terms),
                    lambda: halves(total(wide), 2 + i), (BF, BF),
                )
            else:
                keep, send = split(terms, 2 + i)
            terms = (keep, over_dp(send, bits[i]))
        (out,) = run(sum_body, terms[0].shape[0], (scal, *terms), lambda: (total(terms),))
        for i in range(len(bits) - 1, 0, -1):
            other = over_dp(out, bits[i])
            (out,) = run(
                functools.partial(join_body, at=2 + i), 2 * out.shape[0], (scal, out, other),
                lambda: (joined(out, other, scal[2 + i]),),
            )
        other = over_dp(out, 1)
        body = upper_body if len(outs) == 3 else functools.partial(join_body, at=2)
        if out.shape[0] % TILE:
            both = joined(out, other, scal[2]).astype(F32)
            ends = [sum(outs[:k]) for k in range(len(outs) + 1)]
            return tuple(both[a:z] for a, z in zip(ends, ends[1:]))
        return call(
            body, tuple(shape((rows, width), F32) for rows in outs), (scal, out, other), smem=1, us=1.5,
            mib=8, flush=tuple(range(len(outs))),
        )

    def per_device(
        hidden, segment_ids, pad_mask, query_weight, query_bias, key_weight, value_weight,
        value_bias, proj_weight, proj_bias, norm1_gain, norm1_bias, inner_weight, inner_bias,
        outer_weight, outer_bias, norm2_gain, norm2_bias, output_grad,
    ):
        size, width = hidden.shape
        assert size == segment_ids.shape[1]
        n = query_weight.shape[1]
        units = inner_weight.shape[1] // 3
        heads = n // HD
        place = lax.axis_index("dp")
        me = lax.axis_index("mp")
        scal = jnp.stack([place % 2, me] + [(place // bit) % 2 for bit in bits]).astype(jnp.int32)

        third = 4 * n // 3
        column, row = shape((width, units), BF), shape((units, width), BF)
        own, lead, rest, w1_lead, w1_rest, w2_lead, w2_rest, small, own_far = call(
            pack_body,
            (
                shape((4 * n + TILE, width), BF), shape((third, width), BF), shape((third + TILE, width), BF),
                column, column, row, row, shape((8, width), F32), shape((4 * n + TILE, width), BF),
            ),
            (
                scal, query_weight.T, key_weight.T, value_weight.T, proj_weight, inner_weight, outer_weight,
                query_bias, value_bias, inner_bias, proj_bias, norm1_gain, norm1_bias, outer_bias, norm2_gain, norm2_bias,
            ),
            [pltpu.SemaphoreType.DMA((1,))], smem=1, plain=tuple(range(1, 16)), far=(8,), us=2.0, mib=14,
        )

        def fetch(lead, rest):
            got = over_mp(lead, 2)
            far = (got, over_dp(got, 1), over_mp(rest, 2))
            return far, tuple(over_mp(t, 1) for t in far)

        sib = over_mp(own, 1)
        w1_sib = over_mp(inner_weight, 1)
        w2_sib = over_mp(outer_weight, 1)
        far_a, sib_a = fetch(lead, rest)
        far_1, sib_1 = fetch(w1_lead, w1_rest)
        far_2, sib_2 = fetch(w2_lead, w2_rest)

        pads = size + 2 * MOST
        att_scratch = [
            VMEM((pads, width), BF), VMEM((pads, QB), F32), VMEM((size // QB, WIN, QB), F32), VMEM((pads, HD), BF),
        ]
        work = saved_scratch(n, size, pads, heads)
        pack_scratch = [VMEM((4 * n, width), BF)]
        saved = (shape((n, size), BF), shape((2 * n, pads), BF), shape((n, size), BF), shape((heads, 1, size), F32))
        full = shape((size, width), F32)
        half_full = shape((size, width), BF)
        b1_shape = shape((3, 1, units), F32)
        pack_shape = shape((4 * n, width), BF)
        rows = (scal, segment_ids, pad_mask, hidden)
        *saved0, acc, b1_0 = call(
            near_attention, saved + (full, b1_shape), rows + (own,), att_scratch + work, smem=1, far=(0, 1, 2, 3),
            us=5.0,
        )
        *saved1, acc, b1_1 = call(
            near_attention, saved + (full, b1_shape), rows + (sib, acc), att_scratch + work, smem=1, far=(0, 1, 2, 3),
            us=5.0,
        )
        *saved2, pack2, b1_2, acc = call(
            functools.partial(far_attention, last=False), saved + (pack_shape, b1_shape, full), rows + (*far_a, acc),
            pack_scratch + att_scratch + work, smem=1, far=(0, 1, 2, 3, 4), us=5.0,
        )
        *saved3, pack3, b1_3, first, low, normed, scale = call(
            functools.partial(far_attention, last=True),
            saved + (pack_shape, b1_shape, full, half_full, full, shape((size, 128), F32)),
            rows + (*sib_a, acc, small), pack_scratch + att_scratch + work, smem=1, far=(0, 1, 2, 3, 4), flush=(8, 9),
            us=6.0,
        )

        acts = (shape((2, size, 3 * units), BF), shape((2, size, 3 * units), BF))
        square = shape((width, 3 * units), BF)
        sems = pltpu.SemaphoreType.DMA
        in_n, sl_n, ffn = call(
            near_ffn, acts + (full,), (low, inner_weight, w1_sib, outer_weight, w2_sib, b1_0, b1_1),
            ffn_scratch(size, width, units), any_at=(1, 2, 3, 4), far=(0, 1), us=7.0, mib=16,
        )
        in_f, sl_f, output, dz2, dffn, rows2 = call(
            far_ffn,
            acts + (half_full, full, half_full, shape((8, width), F32)),
            (*far_1, *sib_1, *far_2, *sib_2, low, b1_2, b1_3, ffn, first, output_grad, small),
            [VMEM((size, width), F32)] + ffn_scratch(size, width, units), any_at=tuple(range(12)), far=(0, 1), flush=(2,),
            us=10.0, mib=16,
        )

        def outer_grad(acts, index, far):
            some = len(index)
            return call(
                functools.partial(outer_back, index=index, far=far), (shape((3 * units, width), BF),) * some,
                (scal, acts, dffn), [VMEM((some, size, 3 * units), BF), sems((some,))], smem=1, any_at=(1,),
                us=2.0 * some,
            )

        g2 = outer_grad(in_f, (1,), True) + outer_grad(in_f, (0,), True) + outer_grad(in_n, (1, 0), False)
        (w2_grad,) = reduce_quarters(*g2, scal, (3 * units,))

        grads = (square, square, b1_shape, b1_shape)
        g1_3, g1_2, gb_3, gb_2, dh1 = call(
            inner_far, grads + (full,),
            (scal, *far_1, *sib_1, *far_2, *sib_2, sl_f, low, dffn, dz2),
            inner_scratch(size, width, units), smem=1, any_at=tuple(range(1, 14)), us=7.0, mib=18,
        )
        g1_1, g1_0, gb_1, gb_0, dz1, dattn, rows1 = call(
            inner_near, grads + (full, half_full, shape((8, width), F32)),
            (scal, inner_weight, w1_sib, outer_weight, w2_sib, sl_n, normed, scale, low, dffn, dh1, small),
            [VMEM((size, width), F32), VMEM((size, width), F32), VMEM((size, 128), F32), sems((2,))]
            + inner_scratch(size, width, units), smem=1, any_at=tuple(range(1, 8)), us=9.0, mib=18,
        )
        (w1_grad,) = reduce_quarters(g1_3, g1_2, g1_1, g1_0, scal, (width,))

        tall = 2 * n + TILE
        tall += -tall % (dp * TILE)

        def att_back(grad, gb, pack, saved, final=()):
            return call(
                attention_back, (shape((tall, width), BF), shape((2 * n, width), BF), full),
                rows + (dattn, grad, rows1, rows2, gb, pack) + tuple(saved),
                att_scratch
                + [
                    VMEM((pads, HD), BF), VMEM((3 * n, size), BF), VMEM((HD, pads), F32), VMEM((HD, pads), F32),
                    VMEM((n, size), BF), VMEM((TILE, width), F32),
                ],
                smem=1, flush=final, us=6.0, mib=12,
            )

        up_3, low_3, grad = att_back(dz1, gb_3, pack3, saved3)
        up_2, low_2, grad = att_back(grad, gb_2, pack2, saved2)
        up_1, low_1, grad = att_back(grad, gb_1, sib, saved1)
        up_0, low_0, input_grad = att_back(grad, gb_0, own_far, saved0, (2,))
        gq, gk, vec = reduce_quarters(up_3, up_2, up_1, up_0, scal, (n, n, 8))
        gv, go = reduce_quarters(low_3, low_2, low_1, low_0, scal, (n, n))
        return (
            output,
            input_grad,
            gq.T,
            vec[0, :n],
            gk.T,
            gv.T,
            vec[0, 2 * n : 3 * n],
            go,
            vec[2],
            vec[3],
            vec[4],
            w1_grad,
            vec[1],
            w2_grad,
            vec[5],
            vec[6],
            vec[7],
        )

    return per_device


def solution(mesh):
    rows, cols, rep = P(("dp", "mp"), None), P(None, "mp"), P()
    vec, up = P("mp"), P("mp", None)
    return jax.shard_map(
        build(mesh.shape["dp"], mesh.shape["mp"]),
        mesh=mesh,
        in_specs=(
            rows, P("dp", None), P("dp", None), cols, vec, cols, cols, vec, up, rep,
            rep, rep, cols, vec, up, rep, rep, rep, rows,
        ),
        out_specs=(
            rows, rows, cols, vec, cols, cols, vec, up, rep, rep, rep, cols, vec, up, rep, rep, rep,
        ),
        check_vma=False,
    )
```

```python
import functools
import math

import jax
import jax.numpy as jnp
from jax import lax
from jax.experimental import pallas as pl
from jax.experimental.pallas import tpu as pltpu
from jax.sharding import PartitionSpec as P


HD = 64
MOST = 64
QB = 128
WIN = QB + 2 * MOST
TILE = 16
EPS = 1e-12
BF = jnp.bfloat16
F32 = jnp.float32
SMEM = pltpu.SMEM
VMEM = pltpu.VMEM


def dot_nn(left, right):
    return lax.dot_general(left, right, (((1,), (0,)), ((), ())), preferred_element_type=F32)


def dot_nt(left, right):
    return lax.dot_general(left, right, (((1,), (1,)), ((), ())), preferred_element_type=F32)


def dot_tn(left, right):
    return lax.dot_general(left, right, (((0,), (0,)), ((), ())), preferred_element_type=F32)


def shape(dims, kind):
    return jax.ShapeDtypeStruct(dims, kind)


def call(body, outs, ins, scratch=(), smem=0, any_at=(), plain=(), far=(), flush=(), us=10.0, mib=10):
    def spec(i):
        if i < smem:
            return pl.BlockSpec(memory_space=SMEM)
        if i in any_at:
            return pl.BlockSpec(memory_space=pltpu.HBM)
        return pl.BlockSpec(memory_space=VMEM)

    held = [(pltpu.HBM if i in far or i in flush else VMEM)(o.shape, o.dtype) for i, o in enumerate(outs)]
    ins = [
        x if i < smem else pltpu.with_memory_space_constraint(x, pltpu.HBM if i in plain or i in any_at else VMEM)
        for i, x in enumerate(ins)
    ]
    return pl.pallas_call(
        body,
        out_shape=tuple(held),
        in_specs=[spec(i) for i in range(len(ins))],
        out_specs=tuple(pl.BlockSpec(memory_space=pltpu.HBM if i in far else VMEM) for i in range(len(outs))),
        scratch_shapes=list(scratch),
        compiler_params=pltpu.CompilerParams(vmem_limit_bytes=mib << 20),
        cost_estimate=pl.CostEstimate(flops=int(us * 1e9), transcendentals=0, bytes_accessed=0),
    )(*ins)


def pack_body(
    scal, wq, wk, wv, wo, w1, w2, bq, bv, b1, pb, g1, s1, ob, g2, s2,
    own, lead, rest, w1_lead, w1_rest, w2_lead, w2_rest, small, own_far, sem,
):
    b = scal[0]
    n = wq.shape[0]
    third = lead.shape[0]
    units = w2_lead.shape[0]
    first = pl.multiple_of(b * units, units)
    small[...] = jnp.zeros_like(small)
    small[0, :n] = bq[...].astype(F32)
    small[0, 2 * n : 3 * n] = bv[...].astype(F32)
    for i, ref in enumerate((b1, pb, g1, s1, ob, g2, s2)):
        small[i + 1, :] = ref[...].astype(F32)
    for i, ref in enumerate((wq, wk, wv, wo)):
        own[i * n : (i + 1) * n, :] = ref[...]
    row = small[1:2, :]
    turned = jnp.concatenate([row[:, units : 2 * units], row[:, :units], row[:, 2 * units :]], 1)
    own[4 * n :, :] = jnp.concatenate(
        [small[0:1, :], jnp.where(b == 0, row, turned), row, jnp.zeros((TILE - 3, small.shape[1]), F32)], 0
    ).astype(BF)
    far = pltpu.make_async_copy(own, own_far, sem.at[0])
    far.start()
    lead[...] = own[pl.ds(pl.multiple_of(b * third, third), third), :]
    rest[...] = own[2 * third :, :]
    w1_lead[...] = w1[:, pl.ds(first, units)]
    w2_lead[...] = w2[pl.ds(first, units), :]
    w1_rest[...] = w1[:, 2 * units :]
    w2_rest[...] = w2[2 * units :, :]
    far.wait()


def prepare(scal, seg_ref, pad_ref, hidden, hid, code):
    size = hidden.shape[0]
    me = scal[1]
    zero = jnp.zeros((MOST, hidden.shape[1]), BF)
    hid[:MOST, :] = zero
    hid[MOST : MOST + size, :] = hidden[...]
    hid[MOST + size :, :] = zero
    seg = seg_ref[pl.ds(me, 1), :].astype(F32)
    valid = pad_ref[pl.ds(me, 1), :]
    keys = jnp.where(valid > 0, seg, -1.0)
    empty = jnp.full((MOST, QB), -1.0, F32)
    code[:MOST, :] = empty
    code[MOST : MOST + size, :] = jnp.transpose(jnp.broadcast_to(keys, (QB, size)))
    code[MOST + size :, :] = empty
    return seg


def block_masks(seg, code, masks):
    diagonal = lax.broadcasted_iota(jnp.int32, (WIN, QB), 0) == MOST + lax.broadcasted_iota(
        jnp.int32, (WIN, QB), 1
    )
    for i in range(masks.shape[0]):
        same = code[i * QB : i * QB + WIN, :] == seg[:, i * QB : (i + 1) * QB]
        masks[i] = jnp.where(same | diagonal, 1.0, 0.0)


def column(row):
    return jnp.transpose(jnp.broadcast_to(row, (QB, row.shape[1])))


def bias_column(pack_tail, start, n):
    wide = -(-(start + n) // QB) * QB
    return column(pack_tail[0:1, :wide].astype(F32))[start : start + n]


def saved_scratch(n, size, pads, heads):
    return [
        VMEM((n, size), BF), VMEM((2 * n, pads), BF), VMEM((n, size), BF), VMEM((heads, 1, size), F32),
        pltpu.SemaphoreType.DMA((8,)),
    ]


def attend_quarter(w, tail, hidden, hid, masks, saved, work, ktok):
    qt, kvt, ctxt, lse, sems = work
    copies = [pltpu.make_async_copy(src, dst, sems.at[i]) for i, (src, dst) in enumerate(zip(work[:4], saved))]
    size = hidden.shape[0]
    n = w.shape[0] // 4
    reps = size // QB
    bq = bias_column(tail, 0, n)
    bv = bias_column(tail, 2 * n, n)
    q = dot_nt(w[0:n, :], hidden[...])
    qt[...] = ((q + jnp.concatenate([bq] * reps, 1)).astype(BF).astype(F32) * (1.0 / math.sqrt(HD))).astype(BF)
    kvt[:n, :] = dot_nt(w[n : 2 * n, :], hid[...]).astype(BF)
    kvt[n:, :] = (dot_nt(w[2 * n : 3 * n, :], hid[...]) + jnp.concatenate([bv] * (reps + 1), 1)).astype(BF)
    copies[0].start()
    copies[1].start()

    def head(h, carry):
        at = pl.multiple_of(h * HD, HD)
        ktok[...] = jnp.transpose(kvt[pl.ds(at, HD), :])
        for i in range(reps):
            lanes = slice(i * QB, (i + 1) * QB)
            keys = slice(i * QB, i * QB + WIN)
            s = dot_nn(ktok[keys, :], qt[pl.ds(at, HD), lanes])
            s = jnp.where(masks[i] > 0.0, s, F32(-1000000000.0))
            top = jnp.max(s, 0, keepdims=True)
            e = jnp.exp(s - top)
            total = jnp.sum(e, 0, keepdims=True)
            p = (e * (1.0 / total)).astype(BF)
            ctxt[pl.ds(at, HD), lanes] = dot_nn(kvt[pl.ds(n + at, HD), keys], p).astype(BF)
            lse[h, :, lanes] = top + jnp.log(total)
        return carry

    lax.fori_loop(0, n // HD, head, 0)
    copies[2].start()
    copies[3].start()
    return dot_tn(ctxt[...], w[3 * n : 4 * n, :]), copies


def near_attention(scal, seg_ref, pad_ref, hidden, pack, *refs):
    before, refs = refs[:-15], refs[-15:]
    saved, (acc, b1), (hid, code, masks, ktok), work = refs[:4], refs[4:6], refs[6:10], refs[10:]
    seg = prepare(scal, seg_ref, pad_ref, hidden, hid, code)
    block_masks(seg, code, masks)
    n = pack.shape[0] // 4 // TILE * TILE
    tail = pack.at[4 * n :]
    spread_bias(tail, 2, b1)
    part, copies = attend_quarter(pack.at[: 4 * n], tail, hidden, hid, masks, saved, work, ktok)
    acc[...] = part + before[0][...] if before else part
    for c in copies:
        c.wait()


def spread_bias(tail, row, out):
    units = out.shape[2]
    for k in range(out.shape[0]):
        out[k] = tail[row : row + 1, k * units : (k + 1) * units].astype(F32)


def order(b, lead, other, rest, out):
    size = lead.shape[0]
    out[pl.ds(pl.multiple_of(b * size, size), size), :] = lead[...]
    out[pl.ds(pl.multiple_of((1 - b) * size, size), size), :] = other[...]
    out[2 * size :, :] = rest[: out.shape[0] - 2 * size, :]


def stats(z):
    center = z - jnp.mean(z, -1, keepdims=True)
    scale = lax.rsqrt(jnp.mean(center * center, -1, keepdims=True) + EPS)
    return center * scale, scale


def far_attention(scal, seg_ref, pad_ref, hidden, lead, other, rest, before, *refs, last):
    small = refs[0] if last else None
    refs = refs[1:] if last else refs
    saved, (pack_out, b1), more = refs[:4], refs[4:6], refs[6:-10]
    pack, hid, code, masks, ktok = refs[-10:-5]
    work = refs[-5:]
    seg = prepare(scal, seg_ref, pad_ref, hidden, hid, code)
    block_masks(seg, code, masks)
    order(scal[0], lead, other, rest, pack)
    sems = work[4]
    outs = [pltpu.make_async_copy(pack, pack_out, sems.at[4])]
    outs[0].start()
    tail = rest.at[rest.shape[0] - TILE :]
    spread_bias(tail, 1, b1)
    part, copies = attend_quarter(pack, tail, hidden, hid, masks, saved, work, ktok)
    outs += copies
    total = before[...] + part
    if last:
        first, low, normed, scale = more
        normed[...] = total

        def norm(i, carry):
            at = pl.ds(pl.multiple_of(i * STEP, STEP), STEP)
            unit, r = stats(hidden[at, :].astype(F32) + normed[at, :] + small[2:3, :])
            h1 = unit * small[3:4, :] + small[4:5, :]
            first[at, :] = h1
            low[at, :] = h1.astype(BF)
            normed[at, :] = unit
            scale[at, :] = jnp.broadcast_to(r, (STEP, scale.shape[1]))
            return carry

        lax.fori_loop(0, hidden.shape[0] // STEP, norm, 0)
    else:
        more[0][...] = total
    for c in outs:
        c.wait()


def attention_back(
    scal, seg_ref, pad_ref, hidden, dattn, grad, rows1, rows2, gb, pack, qt, kvt, ctxt, lse,
    upper, lower, acc, hid, code, masks, ktok, vtok, dqkv, dk, dv, dctx, tile,
):
    size = hidden.shape[0]
    reps = size // QB
    seg = prepare(scal, seg_ref, pad_ref, hidden, hid, code)
    block_masks(seg, code, masks)
    n = pack.shape[0] // 4 // TILE * TILE
    dctx[...] = dot_nt(pack[3 * n : 4 * n, :], dattn[...]).astype(BF)
    lower[n:, :] = dot_nn(ctxt[...], dattn[...]).astype(BF)

    def head(h, carry):
        at = pl.multiple_of(h * HD, HD)
        ktok[...] = jnp.transpose(kvt[pl.ds(at, HD), :])
        vtok[...] = jnp.transpose(kvt[pl.ds(n + at, HD), :])
        dk[...] = jnp.zeros_like(dk)
        dv[...] = jnp.zeros_like(dv)
        for i in range(reps):
            lanes = slice(i * QB, (i + 1) * QB)
            keys = slice(i * QB, i * QB + WIN)
            q = qt[pl.ds(at, HD), lanes]
            g = dctx[pl.ds(at, HD), lanes]
            s = dot_nn(ktok[keys, :], q)
            p = jnp.where(masks[i] > 0.0, jnp.exp(s - lse[h, :, lanes]), 0.0)
            dp = dot_nn(vtok[keys, :], g)
            delta = jnp.sum(p * dp, 0, keepdims=True)
            ds = (p * (dp - delta)).astype(BF)
            dq = dot_nn(kvt[pl.ds(at, HD), keys], ds) * (1.0 / math.sqrt(HD))
            dqkv[pl.ds(at, HD), lanes] = dq.astype(BF)
            dk[:, keys] += dot_nt(q, ds)
            dv[:, keys] += dot_nt(g, p.astype(BF))
        wide = dk.shape[1]
        dqkv[pl.ds(n + at, HD), :] = pltpu.roll(dk[...], wide - MOST, 1)[:, :size].astype(BF)
        dqkv[pl.ds(2 * n + at, HD), :] = pltpu.roll(dv[...], wide - MOST, 1)[:, :size].astype(BF)
        return carry

    lax.fori_loop(0, n // HD, head, 0)
    upper[: 2 * n, :] = dot_nn(dqkv[: 2 * n, :], hidden[...]).astype(BF)
    lower[:n, :] = dot_nn(dqkv[2 * n :, :], hidden[...]).astype(BF)
    acc[...] = grad[...] + dot_tn(dqkv[...], pack[: 3 * n, :])
    bias = dot_nt(jnp.ones((8, size), BF), dqkv[...])
    units = gb.shape[2]
    tile[...] = jnp.zeros_like(tile)
    tile[0:1, :n] = bias[0:1, :n]
    tile[0:1, 2 * n : 3 * n] = bias[0:1, 2 * n :]
    for k in range(gb.shape[0]):
        tile[1:2, k * units : (k + 1) * units] = gb[k]
    tile[2:5, :] = rows1[0:3, :]
    tile[5:8, :] = rows2[0:3, :]
    upper[2 * n :, :] = jnp.zeros((upper.shape[0] - 2 * n, upper.shape[1]), BF)
    upper[2 * n : 2 * n + TILE, :] = tile[...].astype(BF)


TAIL = (
    0.11762539007438957, 0.046694333975460314, 0.3222211738117182, -0.31396123834780804, 0.440880529781562,
    -0.11346019315654339,
)
TAIL_P = 0.27599385522864645


def gelu_pair(x):
    t = 1.0 / (1.0 + TAIL_P * jnp.abs(x))
    e = jnp.exp2((x * x) * (-0.5 / math.log(2.0)))
    g = F32(TAIL[-1])
    for c in TAIL[-2::-1]:
        g = g * t + c
    g = g * (t * e)
    phi = jnp.where(x >= 0.0, 1.0 - g, g)
    return x * phi, phi + x * (e * (1.0 / math.sqrt(2.0 * math.pi)))


def quarter_copies(w1, w2, b1, b2, sems):
    if len(w1) == 1:
        parts = [(w1[0], b1), (w2[0], b2)]
    else:
        u = b2.shape[0] // 3
        parts = [(w, b1.at[:, k * u : (k + 1) * u]) for k, w in enumerate(w1)]
        parts += [(w, b2.at[k * u : (k + 1) * u, :]) for k, w in enumerate(w2)]
    copies = [pltpu.make_async_copy(src, dst, sems.at[i]) for i, (src, dst) in enumerate(parts)]
    n = len(w1)
    return copies[:n], copies[n:]


ROWS = 256


def ffn_scratch(size, width, units):
    return [
        VMEM((2, width, 3 * units), BF), VMEM((2, 3 * units, width), BF), VMEM((2, size, 3 * units), BF),
        VMEM((2, size, 3 * units), BF), VMEM((2, 8, 3 * units), F32), pltpu.SemaphoreType.DMA((2, 6)),
        pltpu.SemaphoreType.DMA((4,)),
    ]


def inner_scratch(size, width, units):
    return [
        VMEM((width, size), BF), VMEM((size, 3 * units), BF), VMEM((2, width, 3 * units), BF),
        VMEM((2, 3 * units, width), BF), VMEM((2, size, 3 * units), BF), VMEM((2, width, 3 * units), BF),
        VMEM((2, 3, 1, units), F32), pltpu.SemaphoreType.DMA((2, 7)),
    ]


def ffn_pair(weights, biases, low, start, acc, inner, slope, w1_buf, w2_buf, in_buf, sl_buf, bias_buf, sems, out_sems):
    copies = [
        quarter_copies(w1, w2, w1_buf.at[j], w2_buf.at[j], sems.at[j]) for j, (w1, w2) in enumerate(weights)
    ]
    for first, second in copies:
        for c in first + second:
            c.start()
    both = biases[0].shape[0]
    for k in range(both):
        for j, b1 in enumerate(biases):
            u = b1.shape[2]
            bias_buf[j, 0:1, k * u : (k + 1) * u] = b1[k]
    acc[...] = jnp.zeros_like(acc) if start is None else start[...]
    n = len(copies[0][0])

    def waits(j, at, dst):
        u = dst.shape[2] // 3 if at == 0 else dst.shape[1] // 3
        for k in range(n):
            if n == 1:
                part = dst.at[j]
            else:
                part = dst.at[j, :, k * u : (k + 1) * u] if at == 0 else dst.at[j, k * u : (k + 1) * u, :]
            pltpu.make_async_copy(part, part, sems.at[j, at * n + k]).wait()

    def quarter(j, carry):
        waits(j, 0, w1_buf)

        def gelu(r, carry):
            rows = pl.ds(pl.multiple_of(r * ROWS, ROWS), ROWS)
            act, der = gelu_pair(dot_nn(low[rows, :], w1_buf[j]) + bias_buf[j, 0:1, :])
            in_buf[j, rows, :] = act.astype(BF)
            sl_buf[j, rows, :] = der.astype(BF)
            return carry

        lax.fori_loop(0, low.shape[0] // ROWS, gelu, 0)
        waits(j, 1, w2_buf)
        for i, (buf, out) in enumerate(((in_buf, inner), (sl_buf, slope))):
            pltpu.make_async_copy(buf.at[j], out.at[j], out_sems.at[2 * j + i]).start()
        acc[...] += dot_nn(in_buf[j], w2_buf[j])
        return carry

    lax.fori_loop(0, 2, quarter, 0)
    return [
        pltpu.make_async_copy(buf.at[j], out.at[j], out_sems.at[2 * j + i])
        for j in range(2)
        for i, (buf, out) in enumerate(((in_buf, inner), (sl_buf, slope)))
    ]


def near_ffn(low, w1a, w1b, w2a, w2b, b1_a, b1_b, inner, slope, acc, *scratch):
    outs = ffn_pair([((w1a,), (w2a,)), ((w1b,), (w2b,))], (b1_a, b1_b), low, None, acc, inner, slope, *scratch)
    for c in outs:
        c.wait()


def norm_back(grad, unit, r, gain):
    scaled = grad * gain
    m1 = jnp.mean(scaled, -1, keepdims=True)
    m2 = jnp.mean(scaled * unit, -1, keepdims=True)
    return r * (scaled - m1 - unit * m2)


def row_sums(rows, at, *terms):
    for i, t in enumerate(terms):
        total = jnp.sum(t, 0, keepdims=True)
        rows[i : i + 1, :] = total if at == 0 else rows[i : i + 1, :] + total


STEP = 256


def far_ffn(
    w1a0, w1a1, w1a2, w1b0, w1b1, w1b2, w2a0, w2a1, w2a2, w2b0, w2b1, w2b2, low, b1_a, b1_b, near, first, cot, small,
    inner, slope, out, dz, dffn, rows, acc, *scratch,
):
    outs = ffn_pair(
        [((w1a0, w1a1, w1a2), (w2a0, w2a1, w2a2)), ((w1b0, w1b1, w1b2), (w2b0, w2b1, w2b2))], (b1_a, b1_b), low, near,
        acc, inner, slope, *scratch,
    )
    rows[...] = jnp.zeros_like(rows)

    def norm(i, carry):
        at = pl.ds(pl.multiple_of(i * STEP, STEP), STEP)
        unit, r = stats(first[at, :] + acc[at, :] + small[5:6, :])
        out[at, :] = (unit * small[6:7, :] + small[7:8, :]).astype(BF)
        g = cot[at, :].astype(F32)
        d = norm_back(g, unit, r, small[6:7, :])
        dz[at, :] = d
        d = d.astype(BF)
        dffn[at, :] = d
        row_sums(rows, 1, d.astype(F32), g * unit, g)
        return carry

    lax.fori_loop(0, low.shape[0] // STEP, norm, 0)
    for c in outs:
        c.wait()


def spots(b, far):
    return [b, 1 - b, 2] if far else [0, 1, 2]


def third(k, u):
    return pl.ds(pl.multiple_of(k * u, u), u)


def outer_back(scal, acts, dffn, *refs, index, far):
    outs, (buf, sems) = refs[:-2], refs[-2:]
    copies = [pltpu.make_async_copy(acts.at[k], buf.at[i], sems.at[i]) for i, k in enumerate(index)]
    for c in copies:
        c.start()
    u = outs[0].shape[0] // 3

    def quarter(j, carry):
        pltpu.make_async_copy(buf.at[j], buf.at[j], sems.at[j]).wait()
        grad = dot_tn(buf[j], dffn[...]).astype(BF)
        buf_out = outs[0] if len(outs) == 1 else None
        if buf_out is not None:
            for k, spot in enumerate(spots(scal[0], far)):
                buf_out[third(spot, u), :] = grad[k * u : (k + 1) * u, :]
        else:
            for i, out in enumerate(outs):

                @pl.when(j == i)
                def _(out=out):
                    out[...] = grad

        return carry

    lax.fori_loop(0, len(index), quarter, 0)


def inner_pair(
    scal, weights, far, slope, low, dffn, start, sent, kept, gb_s, gb_k, acc, low_t, dpre, w1_buf, w2_buf, sl_buf, both, gb_both, sems,
):
    copies = []
    for j, (w1, w2) in enumerate(weights):
        first, second = quarter_copies(w1, w2, w1_buf.at[j], w2_buf.at[j], sems.at[j])
        copies.append((second + [pltpu.make_async_copy(slope.at[1 - j], sl_buf.at[j], sems.at[j, 6])], first))
        for c in copies[j][0] + first:
            c.start()
    low_t[...] = jnp.transpose(low[...])
    acc[...] = start[...]
    n = len(weights[0][0])
    place = spots(scal[0], far)
    u = sent.shape[1] // 3

    def waits(j, at, dst):
        for k in range(n):
            if n == 1:
                part = dst.at[j]
            else:
                part = dst.at[j, :, k * u : (k + 1) * u] if at == 0 else dst.at[j, k * u : (k + 1) * u, :]
            pltpu.make_async_copy(part, part, sems.at[j, at * n + k]).wait()

    def quarter(j, carry):
        waits(j, 1, w2_buf)
        pltpu.make_async_copy(slope.at[0], sl_buf.at[j], sems.at[j, 6]).wait()
        d = (dot_nt(dffn[...], w2_buf[j]) * sl_buf[j].astype(F32)).astype(BF)
        dpre[...] = d
        grad = dot_nn(low_t[...], dpre[...]).astype(BF)
        bias = jnp.sum(d.astype(F32), 0, keepdims=True)
        for k, spot in enumerate(place):
            both[j, :, third(spot, u)] = grad[:, k * u : (k + 1) * u]
            gb_both[j, spot] = bias[:, k * u : (k + 1) * u]
        waits(j, 0, w1_buf)
        acc[...] += dot_nt(dpre[...], w1_buf[j])
        return carry

    lax.fori_loop(0, 2, quarter, 0)
    sent[...] = both[0]
    kept[...] = both[1]
    gb_s[...] = gb_both[0]
    gb_k[...] = gb_both[1]


def inner_far(
    scal, w1a0, w1a1, w1a2, w1b0, w1b1, w1b2, w2a0, w2a1, w2a2, w2b0, w2b1, w2b2, slope, low, dffn, dz,
    sent, kept, gb_s, gb_k, acc, *scratch,
):
    weights = [((w1b0, w1b1, w1b2), (w2b0, w2b1, w2b2)), ((w1a0, w1a1, w1a2), (w2a0, w2a1, w2a2))]
    inner_pair(scal, weights, True, slope, low, dffn, dz, sent, kept, gb_s, gb_k, acc, *scratch)


def inner_near(
    scal, w1a, w1b, w2a, w2b, slope, normed_far, scale_far, low, dffn, dz, small,
    sent, kept, gb_s, gb_k, dz1, dattn, rows, acc, normed, scale, norm_sems, *scratch,
):
    copies = [
        pltpu.make_async_copy(normed_far, normed, norm_sems.at[0]), pltpu.make_async_copy(scale_far, scale, norm_sems.at[1])
    ]
    for c in copies:
        c.start()
    weights = [((w1b,), (w2b,)), ((w1a,), (w2a,))]
    inner_pair(scal, weights, False, slope, low, dffn, dz, sent, kept, gb_s, gb_k, acc, *scratch)
    for c in copies:
        c.wait()
    rows[...] = jnp.zeros_like(rows)

    def norm(i, carry):
        at = pl.ds(pl.multiple_of(i * STEP, STEP), STEP)
        grad = acc[at, :]
        unit = normed[at, :]
        d = norm_back(grad, unit, scale[at, 0:1], small[3:4, :])
        dz1[at, :] = d
        d = d.astype(BF)
        dattn[at, :] = d
        row_sums(rows, 1, d.astype(F32), grad * unit, grad)
        return carry

    lax.fori_loop(0, low.shape[0] // STEP, norm, 0)


def swap(x, axis, bit, size):
    return lax.ppermute(x, axis, [(i, i ^ bit) for i in range(size)])


def total(terms):
    return sum(t.astype(F32) for t in terms).astype(BF)


def half(x, index):
    size = x.shape[0] // 2
    return lax.dynamic_slice_in_dim(x, index * size, size, 0)


def joined(mine, other, index):
    twice = jnp.concatenate([mine, mine], 0)
    return lax.dynamic_update_slice_in_dim(twice, other, (1 - index) * mine.shape[0], 0)


def sweep(rows, body):
    step = math.gcd(rows, 64)

    def one(i, carry):
        body(i * step, step)
        return carry

    lax.fori_loop(0, rows // step, one, 0)


def span(at, size):
    return pl.ds(pl.multiple_of(at, math.gcd(size, 64)), size)


def near_body(scal, x, y, z, out):
    size = out.shape[0]

    def body(at, step):
        rows, wide = span(at, step), span((1 - scal[0]) * size + at, step)
        out[rows, :] = total([x[wide, :], y[wide, :], z[rows, :]])

    sweep(size, body)


def first_body(scal, x, y, z, w, keep, send, *, at):
    size = keep.shape[0]
    for out, i in ((keep, scal[at]), (send, 1 - scal[at])):

        def body(start, step, out=out, i=i):
            rows, wide = span(i * size + start, step), span((2 * scal[0] + i) * size + start, step)
            out[span(start, step), :] = total([x[wide, :], y[wide, :], z[rows, :], w[rows, :]])

        sweep(size, body)


def next_body(scal, *refs, at):
    terms, (keep, send) = refs[:-2], refs[-2:]
    size = keep.shape[0]
    for out, i in ((keep, scal[at]), (send, 1 - scal[at])):

        def body(start, step, out=out, i=i):
            rows = span(i * size + start, step)
            out[span(start, step), :] = total([t[rows, :] for t in terms])

        sweep(size, body)


def sum_body(scal, *refs):
    def body(at, step):
        refs[-1][span(at, step), :] = total([t[span(at, step), :] for t in refs[:-1]])

    sweep(refs[-1].shape[0], body)


def join_body(scal, mine, other, *outs, at):
    size = mine.shape[0]
    i = scal[at]

    def body(start, step):
        rows = span(start, step)
        pair = mine[rows, :], other[rows, :]
        if len(outs) == 2:
            pair = [t.astype(F32) for t in pair]
            outs[0][rows, :] = jnp.where(i == 0, *pair)
            outs[1][rows, :] = jnp.where(i == 0, *pair[::-1])
        else:
            for t, k in zip(pair, (i, 1 - i)):
                outs[0][span(k * size + start, step), :] = t.astype(outs[0].dtype)

    sweep(size, body)


def upper_body(scal, mine, other, q, k, *vectors):
    n, size = q.shape[0], mine.shape[0]
    first = scal[2] == 0
    low = jnp.where(first, mine[...].astype(F32), other[...].astype(F32))
    high = jnp.where(first, other[...].astype(F32), mine[...].astype(F32))
    both = [(low, 0), (high, size)]

    def rows(start, stop):
        parts = [ref[max(start, at) - at : min(stop, at + size) - at] for ref, at in both if start < at + size and stop > at]
        return parts[0] if len(parts) == 1 else jnp.concatenate(parts, 0)

    q[...] = rows(0, n)
    k[...] = rows(n, 2 * n)
    tile = rows(2 * n, 2 * n + 8)
    vectors[0][...] = tile[0, :n]
    vectors[1][...] = tile[0, 2 * n : 3 * n]
    for i, out in enumerate(vectors[2:]):
        out[...] = tile[1 + i]


def build(dp, mp):
    assert mp == 4 and dp & (dp - 1) == 0
    bits = [1 << i for i in range(dp.bit_length() - 1)]

    def over_mp(x, bit):
        return swap(x, "mp", bit, mp)

    def over_dp(x, bit):
        return swap(x, "dp", bit, dp)

    def reduce_quarters(far_sent, far_kept, near_sent, near_kept, scal, outs):
        width = far_kept.shape[1]

        def run(body, rows, ins, plain, kinds=(BF,), **more):
            if rows % TILE:
                return plain()
            outs = tuple(shape((rows, width), kind) for kind in kinds)
            return call(body, outs, ins, smem=1, us=1.0, mib=6, **more)

        def halves(x, i):
            return half(x, scal[i]), half(x, 1 - scal[i])

        def split(terms, i):
            return run(
                functools.partial(next_body, at=i), terms[0].shape[0] // 2, (scal, *terms),
                lambda: halves(total(terms), i), (BF, BF),
            )

        size = far_kept.shape[0]
        far = (far_kept, over_mp(far_sent, 1))
        ours = (near_kept, over_mp(near_sent, 1))
        keep, send = split(far, 2)
        xb = over_mp(send, 2)
        xa = over_mp(keep, 2)
        plain = [half(t, 1 - scal[0]) for t in ours] + [xb]
        (send,) = run(near_body, size // 2, (scal, *ours, xb), lambda: (total(plain),))
        y = over_dp(send, 1)
        terms = ours + (xa, y)
        for i in range(1, len(bits)):
            if len(terms) == 4:
                wide = [half(t, scal[0]) for t in terms[:2]] + list(terms[2:])
                keep, send = run(
                    functools.partial(first_body, at=2 + i), size // 4, (scal, *terms),
                    lambda: halves(total(wide), 2 + i), (BF, BF),
                )
            else:
                keep, send = split(terms, 2 + i)
            terms = (keep, over_dp(send, bits[i]))
        (out,) = run(sum_body, terms[0].shape[0], (scal, *terms), lambda: (total(terms),))
        for i in range(len(bits) - 1, 0, -1):
            other = over_dp(out, bits[i])
            (out,) = run(
                functools.partial(join_body, at=2 + i), 2 * out.shape[0], (scal, out, other),
                lambda: (joined(out, other, scal[2 + i]),),
            )
        other = over_dp(out, 1)
        body = upper_body if len(outs) > 2 else functools.partial(join_body, at=2)
        if out.shape[0] % TILE:
            both = joined(out, other, scal[2]).astype(F32)
            return tuple(jnp.split(both, len(outs)))
        return call(
            body, tuple(shape(dims, F32) for dims in outs), (scal, out, other), smem=1, us=1.5,
            mib=8, flush=tuple(range(len(outs))),
        )

    def per_device(
        hidden, segment_ids, pad_mask, query_weight, query_bias, key_weight, value_weight,
        value_bias, proj_weight, proj_bias, norm1_gain, norm1_bias, inner_weight, inner_bias,
        outer_weight, outer_bias, norm2_gain, norm2_bias, output_grad,
    ):
        size, width = hidden.shape
        assert size == segment_ids.shape[1]
        n = query_weight.shape[1]
        units = inner_weight.shape[1] // 3
        heads = n // HD
        place = lax.axis_index("dp")
        me = lax.axis_index("mp")
        scal = jnp.stack([place & 1, me] + [(place >> i) & 1 for i in range(len(bits))]).astype(jnp.int32)

        third = 4 * n // 3
        column, row = shape((width, units), BF), shape((units, width), BF)
        own, lead, rest, w1_lead, w1_rest, w2_lead, w2_rest, small, own_far = call(
            pack_body,
            (
                shape((4 * n + TILE, width), BF), shape((third, width), BF), shape((third + TILE, width), BF),
                column, column, row, row, shape((8, width), F32), shape((4 * n + TILE, width), BF),
            ),
            (
                scal, query_weight.T, key_weight.T, value_weight.T, proj_weight, inner_weight, outer_weight,
                query_bias, value_bias, inner_bias, proj_bias, norm1_gain, norm1_bias, outer_bias, norm2_gain, norm2_bias,
            ),
            [pltpu.SemaphoreType.DMA((1,))], smem=1, plain=tuple(range(1, 16)), far=(8,), us=2.0, mib=14,
        )

        def fetch(lead, rest):
            got = over_mp(lead, 2)
            far = (got, over_dp(got, 1), over_mp(rest, 2))
            return far, tuple(over_mp(t, 1) for t in far)

        sib = over_mp(own, 1)
        w1_sib = over_mp(inner_weight, 1)
        w2_sib = over_mp(outer_weight, 1)
        far_a, sib_a = fetch(lead, rest)
        far_1, sib_1 = fetch(w1_lead, w1_rest)
        far_2, sib_2 = fetch(w2_lead, w2_rest)

        pads = size + 2 * MOST
        att_scratch = [
            VMEM((pads, width), BF), VMEM((pads, QB), F32), VMEM((size // QB, WIN, QB), F32), VMEM((pads, HD), BF),
        ]
        work = saved_scratch(n, size, pads, heads)
        pack_scratch = [VMEM((4 * n, width), BF)]
        saved = (shape((n, size), BF), shape((2 * n, pads), BF), shape((n, size), BF), shape((heads, 1, size), F32))
        full = shape((size, width), F32)
        half_full = shape((size, width), BF)
        b1_shape = shape((3, 1, units), F32)
        pack_shape = shape((4 * n, width), BF)
        rows = (scal, segment_ids, pad_mask, hidden)
        *saved0, acc, b1_0 = call(
            near_attention, saved + (full, b1_shape), rows + (own,), att_scratch + work, smem=1, far=(0, 1, 2, 3),
            us=5.0,
        )
        *saved1, acc, b1_1 = call(
            near_attention, saved + (full, b1_shape), rows + (sib, acc), att_scratch + work, smem=1, far=(0, 1, 2, 3),
            us=5.0,
        )
        *saved2, pack2, b1_2, acc = call(
            functools.partial(far_attention, last=False), saved + (pack_shape, b1_shape, full), rows + (*far_a, acc),
            pack_scratch + att_scratch + work, smem=1, far=(0, 1, 2, 3, 4), us=5.0,
        )
        *saved3, pack3, b1_3, first, low, normed, scale = call(
            functools.partial(far_attention, last=True),
            saved + (pack_shape, b1_shape, full, half_full, full, shape((size, 128), F32)),
            rows + (*sib_a, acc, small), pack_scratch + att_scratch + work, smem=1, far=(0, 1, 2, 3, 4), flush=(8, 9),
            us=6.0,
        )

        acts = (shape((2, size, 3 * units), BF), shape((2, size, 3 * units), BF))
        square = shape((width, 3 * units), BF)
        sems = pltpu.SemaphoreType.DMA
        in_n, sl_n, ffn = call(
            near_ffn, acts + (full,), (low, inner_weight, w1_sib, outer_weight, w2_sib, b1_0, b1_1),
            ffn_scratch(size, width, units), any_at=(1, 2, 3, 4), far=(0, 1), us=7.0, mib=16,
        )
        in_f, sl_f, output, dz2, dffn, rows2 = call(
            far_ffn,
            acts + (half_full, full, half_full, shape((8, width), F32)),
            (*far_1, *sib_1, *far_2, *sib_2, low, b1_2, b1_3, ffn, first, output_grad, small),
            [VMEM((size, width), F32)] + ffn_scratch(size, width, units), any_at=tuple(range(12)), far=(0, 1), flush=(2,),
            us=10.0, mib=16,
        )

        def outer_grad(acts, index, far):
            some = len(index)
            return call(
                functools.partial(outer_back, index=index, far=far), (shape((3 * units, width), BF),) * some,
                (scal, acts, dffn), [VMEM((some, size, 3 * units), BF), sems((some,))], smem=1, any_at=(1,),
                us=2.0 * some,
            )

        g2 = outer_grad(in_f, (1,), True) + outer_grad(in_f, (0,), True) + outer_grad(in_n, (1, 0), False)
        (w2_grad,) = reduce_quarters(*g2, scal, ((3 * units, width),))

        grads = (square, square, b1_shape, b1_shape)
        g1_3, g1_2, gb_3, gb_2, dh1 = call(
            inner_far, grads + (full,),
            (scal, *far_1, *sib_1, *far_2, *sib_2, sl_f, low, dffn, dz2),
            inner_scratch(size, width, units), smem=1, any_at=tuple(range(1, 14)), us=7.0, mib=18,
        )
        g1_1, g1_0, gb_1, gb_0, dz1, dattn, rows1 = call(
            inner_near, grads + (full, half_full, shape((8, width), F32)),
            (scal, inner_weight, w1_sib, outer_weight, w2_sib, sl_n, normed, scale, low, dffn, dh1, small),
            [VMEM((size, width), F32), VMEM((size, width), F32), VMEM((size, 128), F32), sems((2,))]
            + inner_scratch(size, width, units), smem=1, any_at=tuple(range(1, 8)), us=9.0, mib=18,
        )
        (w1_grad,) = reduce_quarters(g1_3, g1_2, g1_1, g1_0, scal, ((width, 3 * units),))

        tall = 2 * n + TILE
        tall += -tall % (dp * TILE)

        def att_back(grad, gb, pack, saved, final=()):
            return call(
                attention_back, (shape((tall, width), BF), shape((2 * n, width), BF), full),
                rows + (dattn, grad, rows1, rows2, gb, pack) + tuple(saved),
                att_scratch
                + [
                    VMEM((pads, HD), BF), VMEM((3 * n, size), BF), VMEM((HD, pads), F32), VMEM((HD, pads), F32),
                    VMEM((n, size), BF), VMEM((TILE, width), F32),
                ],
                smem=1, flush=final, us=6.0, mib=12,
            )

        up_3, low_3, grad = att_back(dz1, gb_3, pack3, saved3)
        up_2, low_2, grad = att_back(grad, gb_2, pack2, saved2)
        up_1, low_1, grad = att_back(grad, gb_1, sib, saved1)
        up_0, low_0, input_grad = att_back(grad, gb_0, own_far, saved0, (2,))
        gq, gk, gbq, gbv, gb1, *whole = reduce_quarters(
            up_3, up_2, up_1, up_0, scal, ((n, width),) * 2 + ((n,),) * 2 + ((width,),) * 7
        )
        gv, go = reduce_quarters(low_3, low_2, low_1, low_0, scal, ((n, width),) * 2)
        return (
            output,
            input_grad,
            gq.T,
            gbq,
            gk.T,
            gv.T,
            gbv,
            go,
            *whole[:3],
            w1_grad,
            gb1,
            w2_grad,
            *whole[3:],
        )

    return per_device


def solution(mesh):
    rows, cols, rep = P(("dp", "mp"), None), P(None, "mp"), P()
    vec, up = P("mp"), P("mp", None)
    return jax.shard_map(
        build(mesh.shape["dp"], mesh.shape["mp"]),
        mesh=mesh,
        in_specs=(
            rows, P("dp", None), P("dp", None), cols, vec, cols, cols, vec, up, rep,
            rep, rep, cols, vec, up, rep, rep, rep, rows,
        ),
        out_specs=(
            rows, rows, cols, vec, cols, cols, vec, up, rep, rep, rep, cols, vec, up, rep, rep, rep,
        ),
        check_vma=False,
    )
```
